512 devices in a mesh: expert: 32 (over x, z), tensor: 8 (over y), dp: 2 (over core).
Axes of the slice: x: 4, y: 8, z: 8, core: 2. Of those that a mesh axis runs over, the one named last changes fastest.
Arguments:
- tokens: bfloat16 [4096, 7168], P(('expert', 'dp'), 'tensor'), may hold values from -6 to 6
- gate_weight: bfloat16 [32, 7168, 1024], P('expert', 'tensor', 'dp'), may hold values from -0.25 to 0.25
- up_weight: bfloat16 [32, 7168, 1024], P('expert', 'tensor', 'dp'), may hold values from -0.25 to 0.25
- down_weight: bfloat16 [32, 1024, 7168], P('expert', 'dp', 'tensor'), may hold values from -0.1875 to 0.1875
- sketch: bfloat16 [32, 2, 1024, 512], P('expert', None, 'dp'), may hold values from -6 to 6
- clusters: int32 [32], replicated, may hold values from 0 to 11, never falling along the last dimension, each value on 1 to 4 neighbouring positions
- routes: int32 [4096, 8], P(('expert', 'dp')), may hold values from 0 to 31, all different within a row; in each aligned block of 64 rows (0 to 63, 64 to 127, ...) at most 24 rows name the same one
- route_weights: float32 [4096, 8], P(('expert', 'dp')), may hold values from 0.05 to 0.3
Outputs:
- mixed: bfloat16 [4096, 7168], P(('expert', 'dp'), 'tensor')
The draws below stay inside these ranges and needn't reach their ends.
Inputs may be any that keep to these rules, and one draw needn't show every extreme that they name: `clusters`: the experts of one cluster are consecutive; a cluster holds 1 to 4 experts, and one holds exactly 4. `routes`: A row names 8 different experts. In each aligned block of 64 rows (the rows of one device) no expert is named by more than 24 rows, a bound that some block reaches.
All inputs are finite; a program needn't handle non-finite values.
Results may differ from the reference program's by a relative error of at most 0.023.
Values may be sent and summed in bfloat16 or wider, within the bound.
A program may use at most 64 MiB of HBM per device.

```python
import math
import jax
import jax.numpy as jnp
import numpy as np
from jax import lax

D = 7168
HID = 1024
RANK = 512
TOP = 8
MOST = 4
TOK_DEV = 64
EXPERTS = 32
CLUSTERS = 12
CAP = 24
TOKENS = 4096
N_EXPERT = 32
N_TENSOR = 8
N_DP = 2


def shard_levels(rng, dims, split, low, high):
    def one(dim, parts):
        heights = jax.random.uniform(jax.random.fold_in(jax.random.fold_in(rng, 6), dim), (parts,), jnp.float32, low / len(split), high / len(split))
        return jnp.repeat(jnp.exp(heights), dims[dim] // parts).reshape((-1,) + (1,) * (len(dims) - dim - 1))

    factor_of = one(*split[0])
    for cut in split[1:]:
        factor_of = factor_of * one(*cut)
    return factor_of


def length_profile(count, total, reach, slope):
    portions = [(1 << 20) // math.isqrt(standing ** slope) + 1 for standing in range(2, count + 1)]
    spare, counts = total - reach - (count - 1), [1] * (count - 1)
    while spare > 0:
        free = [i for i in range(count - 1) if counts[i] < reach]
        pool, remaining = sum([portions[i] for i in free]), spare
        for i in free:
            more = min(reach - counts[i], max(1, remaining * portions[i] // pool), spare)
            counts[i] = counts[i] + more
            spare = spare - more
    return np.array([reach] + counts)


def uneven(rng, amount, total, limit, lean):
    if amount == 2:
        one = jax.random.randint(rng, (), max(1, total - limit), min(limit, total - 1) + 1)
        return jnp.stack([one, total - one])
    lengths = jnp.asarray(length_profile(amount, total, limit, lean), jnp.int32)
    couples = (amount - 1) // 2
    giver, receiver = lengths[1:1 + 2 * couples:2], lengths[2:2 + 2 * couples:2]
    room = jnp.minimum(giver - 1, limit - receiver)
    shifted = jax.random.randint(jax.random.fold_in(rng, 1), (couples,), 0, 1 << 20) % (room + 1)
    lengths = lengths.at[1:1 + 2 * couples:2].set(giver - shifted).at[2:2 + 2 * couples:2].set(receiver + shifted)
    return lengths[jax.random.permutation(jax.random.fold_in(rng, 2), amount)]


def routed_block(stream_key, own, number, rows, amount, top, bound, lean):
    ranking = jax.random.permutation(stream_key, amount)
    heavy_load, common = portions_of(amount, rows * top, bound, lean, True), portions_of(amount, rows * top, bound, lean, False)
    places = jnp.arange(amount)

    def named(lengths, offset_by):
        used = int((lengths > 0).sum())
        fixed = max(1, used // 4)
        passed = fixed + (places - fixed + offset_by * (used - fixed)) % max(1, amount - fixed)
        return jnp.zeros((amount,), jnp.int32).at[ranking[jnp.where(places < fixed, places, passed)]].set(jnp.asarray(lengths, jnp.int32))

    lengths = jnp.where(number % 4 == 0, named(heavy_load, number // 4), named(common, number - number // 4 - 1))
    mixed = jax.random.permutation(jax.random.fold_in(own, 3), amount)
    giver, taker = mixed[0:amount // 2 * 2:2], mixed[1:amount // 2 * 2:2]
    margin = jnp.minimum(lengths[giver] - 1, bound - lengths[taker]) // 2
    margin = jnp.where((giver == ranking[0]) | (taker == ranking[0]) | (lengths[taker] == 0), 0, jnp.maximum(margin, 0))
    passed = jax.random.randint(jax.random.fold_in(own, 4), (amount // 2,), 0, 1 << 20) % (margin + 1)
    lengths = lengths.at[giver].add(-passed).at[taker].add(passed)
    labels = jnp.searchsorted(jnp.cumsum(lengths), jnp.arange(rows * top), side="right").astype(jnp.int32)
    listing = labels.reshape(top, rows).T
    listing = listing[jax.random.permutation(jax.random.fold_in(own, 1), rows)]
    offset_by = jax.random.randint(jax.random.fold_in(own, 2), (rows, 1), 0, top)
    return jnp.take_along_axis(listing, (jnp.arange(top)[None, :] + offset_by) % top, axis=1)


def portions_of(count, total, reach, skew, full):
    loads = [(1 << 20) // math.isqrt(grade ** skew) + 1 for grade in range(1, count + 1)]
    largest = reach if full else min(reach, max(-(-total // count), total * loads[0] // sum(loads)))
    least = 1 if total - largest >= count - 1 else 0
    given, rest = [largest] + [least] * (count - 1), total - largest - least * (count - 1)
    while rest > 0:
        free = [i for i in range(1, count) if given[i] < largest] or [i for i in range(1, count) if given[i] < reach]
        whole, remaining = sum([loads[i] for i in free]), rest
        for i in free:
            extra = min(reach - given[i], max(1, remaining * loads[i] // whole), rest)
            given[i] = given[i] + extra
            rest = rest - extra
    return np.array(given)


def normal_values(rng, shape, scale, reach, cuts=(), kind=jnp.bfloat16):
    level = shard_levels(rng, shape, cuts, -0.22, 0.18) if cuts else 1.0
    array = jax.random.normal(rng, shape, jnp.float32) * scale * level
    return jnp.minimum(jnp.maximum(array, -reach), reach).astype(kind)


def setup_inputs(seed: int = 0) -> dict:
    splits = jax.random.split(jax.random.key(seed), 9)
    tokens = normal_values(splits[0], (TOKENS, D), 1.0, 6.0, ((0, 64), (1, 8)))
    gate_weight = normal_values(splits[1], (EXPERTS, D, HID), RANK ** -0.5, 0.25, ((0, 32), (1, 8), (2, 2)))
    up_weight = normal_values(splits[2], (EXPERTS, D, HID), RANK ** -0.5, 0.25, ((0, 32), (1, 8), (2, 2)))
    down_weight = normal_values(splits[3], (EXPERTS, HID, D), HID ** -0.5, 0.1875, ((0, 32), (1, 2), (2, 8)))
    sketch = normal_values(splits[4], (EXPERTS, 2, HID, RANK), 1.0, 6.0, ((0, 32), (2, 2)))
    clusters = jnp.searchsorted(jnp.cumsum(uneven(splits[5], CLUSTERS, EXPERTS, MOST, 1)), jnp.arange(EXPERTS), side="right").astype(jnp.int32)
    routes_keys = jax.random.split(jax.random.fold_in(splits[6], 1), TOKENS // TOK_DEV)
    routes_turns = jax.random.permutation(jax.random.fold_in(splits[6], 3), TOKENS // TOK_DEV)
    routes = jax.vmap(lambda own, number: routed_block(jax.random.fold_in(splits[6], 2), own, number, TOK_DEV, EXPERTS, TOP, CAP, 2))(routes_keys, routes_turns).reshape((TOKENS, TOP))
    route_weights = jnp.clip(0.05 + 0.25 * jax.random.uniform(splits[7], (TOKENS, TOP), jnp.float32) ** shard_levels(splits[7], (TOKENS, TOP), ((0, 64),), -0.2, 0.2), 0.05, 0.3)
    return dict(tokens=tokens, gate_weight=gate_weight, up_weight=up_weight, down_weight=down_weight, sketch=sketch, clusters=clusters, routes=routes, route_weights=route_weights)


HIGHEST = lax.Precision.HIGHEST

def reference(tokens, gate_weight, up_weight, down_weight, sketch, clusters, routes, route_weights):
    experts = gate_weight.shape[0]
    indices = jnp.arange(experts, dtype=jnp.int32)

    def sketch_one(index):
        return jnp.dot(gate_weight[index].astype(jnp.float32), sketch[index, 0].astype(jnp.float32), preferred_element_type=jnp.float32) + jnp.dot(up_weight[index].astype(jnp.float32), sketch[index, 1].astype(jnp.float32), preferred_element_type=jnp.float32)
    sketched = lax.map(sketch_one, indices)
    same = (clusters[:, None] == clusters[None, :]).astype(jnp.float32)

    def compress(index):
        summed = jnp.tensordot(same[index], sketched, axes=1, precision=HIGHEST)
        gram = lax.dot_general(summed, summed, (((0,), (0,)), ((), ())), precision=HIGHEST)
        factor = jnp.linalg.cholesky(gram)
        basis = jax.scipy.linalg.solve_triangular(factor, summed.T, lower=True).T.astype(jnp.bfloat16)
        blocks = basis.reshape(N_TENSOR, -1, RANK).astype(jnp.float32)
        gate_blocks = gate_weight[index].reshape(N_TENSOR, -1, HID).astype(jnp.float32)
        up_blocks = up_weight[index].reshape(N_TENSOR, -1, HID).astype(jnp.float32)
        gate_parts = jnp.einsum('tdr,tdh->trh', blocks, gate_blocks, precision=HIGHEST).astype(jnp.bfloat16)
        up_parts = jnp.einsum('tdr,tdh->trh', blocks, up_blocks, precision=HIGHEST).astype(jnp.bfloat16)
        gate_parts, up_parts = lax.optimization_barrier((gate_parts, up_parts))
        gate_sum = jnp.sum(gate_parts.astype(jnp.float32), axis=0)
        up_sum = jnp.sum(up_parts.astype(jnp.float32), axis=0)
        return (basis, jnp.stack([gate_sum, up_sum]).astype(jnp.bfloat16))
    bases, coefficients = lax.map(compress, indices)
    targets = routes.reshape(-1)
    total_rows = targets.shape[0]
    top_count = routes.shape[1]
    token_count = tokens.shape[0]
    per_expert = N_EXPERT * N_DP * CAP
    onehot = (targets[:, None] == indices[None, :]).astype(jnp.int32)
    place = jnp.sum((jnp.cumsum(onehot, axis=0) - 1) * onehot, axis=1)
    slot_index = (targets * per_expert + place).astype(jnp.int32)
    owners = jnp.full((experts * per_expert,), token_count, jnp.int32)
    owners = owners.at[slot_index].set(jnp.arange(total_rows, dtype=jnp.int32) // top_count)
    owners = owners.reshape(experts, per_expert)
    padded = jnp.concatenate([tokens, jnp.zeros((1, tokens.shape[1]), jnp.bfloat16)], axis=0)

    def evaluate(index):
        gathered = padded[owners[index]]
        projected = jnp.dot(gathered.astype(jnp.float32), bases[index].astype(jnp.float32), preferred_element_type=jnp.float32).astype(jnp.bfloat16)
        gate_part = jnp.dot(projected.astype(jnp.float32), coefficients[index, 0].astype(jnp.float32), preferred_element_type=jnp.float32)
        up_part = jnp.dot(projected.astype(jnp.float32), coefficients[index, 1].astype(jnp.float32), preferred_element_type=jnp.float32)
        hidden = (jax.nn.silu(gate_part) * up_part).astype(jnp.bfloat16)
        return jnp.dot(hidden.astype(jnp.float32), down_weight[index].astype(jnp.float32), preferred_element_type=jnp.float32).astype(jnp.bfloat16)
    answers = lax.map(evaluate, indices).reshape(experts * per_expert, -1)
    slots = slot_index.reshape(token_count, top_count)
    mixed = jnp.zeros((token_count, tokens.shape[1]), jnp.float32)
    for column in range(top_count):
        mixed = mixed + answers[slots[:, column]].astype(jnp.float32) * route_weights[:, column][:, None]
    return mixed.astype(jnp.bfloat16)
```

```python
import jax
import jax.numpy as jnp
from jax import lax
from jax.experimental import pallas as pl
from jax.experimental.pallas import tpu as pltpu
from jax.sharding import PartitionSpec as P

HIGHEST = lax.Precision.HIGHEST
BLK = 128


def factor_block(tiles):
    lane = lax.broadcasted_iota(jnp.int32, (8, BLK), 1)
    sub = lax.broadcasted_iota(jnp.int32, (8, BLK), 0)
    n = BLK // 8
    tiles = list(tiles)
    for k in range(0, BLK, 2):
        t, r = divmod(k, 8)
        cur = tiles[t]
        col1 = jnp.broadcast_to(cur[:, k:k + 1], (8, BLK))
        col2 = jnp.broadcast_to(cur[:, k + 1:k + 2], (8, BLK))
        a = col1[r:r + 1, :]
        b = col1[r + 1:r + 2, :]
        c = col2[r + 1:r + 2, :]
        ra = 1.0 / a
        rc = a / (a * c - b * b)
        first, second = lane == k, lane == k + 1
        both = jnp.logical_or(first, second)
        row1 = jnp.where(first[:1], 1.0, jnp.where(second[:1], 0.0, cur[r:r + 1, :]))
        row2 = jnp.where(both[:1], 0.0, cur[r + 1:r + 2, :]) - (b * ra) * row1
        row2 = jnp.where(second[:1], 1.0, row2)
        v2 = rc * row2
        v1 = ra * row1 - (b * ra) * v2
        for i in range(t, n):
            old = tiles[i]
            if i == t:
                new = jnp.where(both, 0.0, old) - col1 * v1 - col2 * v2
                new = jnp.where(sub > r + 1, new, old)
                new = jnp.where(sub == r, row1 * jnp.sqrt(ra), new)
                new = jnp.where(sub == r + 1, row2 * jnp.sqrt(rc), new)
            else:
                c1 = jnp.broadcast_to(old[:, k:k + 1], (8, BLK))
                c2 = jnp.broadcast_to(old[:, k + 1:k + 2], (8, BLK))
                new = jnp.where(both, 0.0, old) - c1 * v1 - c2 * v2
            tiles[i] = new
    return [jnp.where(lane <= sub + 8 * i, tiles[i], 0.0) for i in range(n)]

def chol_kernel(g_ref, out_ref, inv_ref):
    size = g_ref.shape[0]
    steps = size // BLK
    out_ref[...] = g_ref[...]

    def step(j, carry):
        at = pl.multiple_of(j * BLK, BLK)
        tiles = [out_ref[pl.ds(pl.multiple_of(at + 8 * i, 8), 8), pl.ds(at, BLK)] for i in range(BLK // 8)]
        for i, tile in enumerate(factor_block(tiles)):
            inv_ref[8 * i:8 * i + 8, :] = tile
        inv = inv_ref[...]
        rows = lax.broadcasted_iota(jnp.int32, (BLK, BLK), 0)
        cols = lax.broadcasted_iota(jnp.int32, (BLK, BLK), 1)
        eye = jnp.where(rows == cols, 1.0, 0.0)
        out_ref[pl.ds(at, BLK), pl.ds(at, BLK)] = eye
        full = jnp.dot(inv, out_ref[pl.ds(at, BLK), :], precision=HIGHEST, preferred_element_type=jnp.float32)
        column = lax.broadcasted_iota(jnp.int32, (BLK, size), 1)
        later = jnp.where(column >= at + BLK, full, 0.0)
        out_ref[pl.ds(at, BLK), :] = full
        column = lax.broadcasted_iota(jnp.int32, (size, size), 1)
        row = lax.broadcasted_iota(jnp.int32, (size, size), 0)
        zero = (column >= at) & (column < at + BLK) & (row >= at + BLK)
        out_ref[...] = jnp.where(zero, 0.0, out_ref[...]) - lax.dot_general(
            later, full, (((0,), (0,)), ((), ())), precision=HIGHEST, preferred_element_type=jnp.float32)
        return carry

    lax.fori_loop(0, steps, step, 0)
    row = lax.broadcasted_iota(jnp.int32, (size, size), 0)
    column = lax.broadcasted_iota(jnp.int32, (size, size), 1)
    out_ref[...] = jnp.where(column <= row, out_ref[...], 0.0)

def inverse_factor(gram):
    size = gram.shape[0]
    return pl.pallas_call(
        chol_kernel,
        out_shape=jax.ShapeDtypeStruct((size, size), jnp.float32),
        in_specs=[pl.BlockSpec(memory_space=pltpu.VMEM)],
        out_specs=pl.BlockSpec(memory_space=pltpu.VMEM),
        scratch_shapes=[pltpu.VMEM((BLK, BLK), jnp.float32)],
        cost_estimate=pl.CostEstimate(flops=4 * size ** 3, bytes_accessed=8 * size * size, transcendentals=0),
    )(gram)

def split_dot(precise, plain, transposed):
    high = precise.astype(jnp.bfloat16)
    low = (precise - high.astype(jnp.float32)).astype(jnp.bfloat16)
    if transposed:
        dims = (((1,), (1,)), ((), ()))
        return lax.dot_general(plain, high, dims, preferred_element_type=jnp.float32) + lax.dot_general(
            plain, low, dims, preferred_element_type=jnp.float32)
    dims = (((1,), (0,)), ((), ()))
    return lax.dot_general(high, plain, dims, preferred_element_type=jnp.float32) + lax.dot_general(
        low, plain, dims, preferred_element_type=jnp.float32)


def sum_over(value, axis):
    count = lax.axis_size(axis)
    pieces = value.reshape((count, value.shape[0] // count) + value.shape[1:])
    arrived = lax.all_to_all(pieces, axis, split_axis=0, concat_axis=0, tiled=True)
    return jnp.sum(arrived.astype(jnp.float32), axis=0)


def transposed_dot(left, right):
    return lax.dot_general(left, right, (((0,), (0,)), ((), ())), preferred_element_type=jnp.float32)


def on_device(tokens, gate_weight, up_weight, down_weight, sketch, clusters, routes, route_weights):
    gate_rows = gate_weight[0]
    up_rows = up_weight[0]
    experts = lax.axis_size("expert")
    half = lax.axis_index("dp")
    sketched = jnp.dot(gate_rows, sketch[0, 0], preferred_element_type=jnp.float32) + jnp.dot(
        up_rows, sketch[0, 1], preferred_element_type=jnp.float32
    )
    rows, rank = sketched.shape
    part = rows // 2
    kept = lax.dynamic_slice_in_dim(sketched, half * part, part, 0)
    sent = lax.dynamic_slice_in_dim(sketched, (1 - half) * part, part, 0).astype(jnp.bfloat16)
    own = kept + lax.ppermute(sent, "dp", [(0, 1), (1, 0)]).astype(jnp.float32)
    across, down = experts // 4, rank // 4
    pieces = own.astype(jnp.bfloat16).reshape(across, part // across, 4, down).transpose(0, 2, 1, 3)
    pieces = pieces.reshape(experts, part // across, down)
    pieces = lax.all_to_all(pieces, "expert", split_axis=0, concat_axis=0, tiled=True)
    same = (clusters[:, None] == clusters[None, :]).astype(jnp.bfloat16)
    pieces = jnp.einsum("ef,frc->erc", same, pieces, preferred_element_type=jnp.float32).astype(jnp.bfloat16)
    pieces = lax.all_to_all(pieces, "expert", split_axis=0, concat_axis=0, tiled=True)
    summed = pieces.reshape(across, 4, part // across, down).transpose(0, 2, 1, 3).reshape(part, rank)
    summed = lax.all_gather(summed, "dp", axis=0, tiled=True)

    columns = lax.dynamic_slice_in_dim(summed, half * (rank // 2), rank // 2, 1)
    gram = sum_over(transposed_dot(summed, columns), "tensor")
    gram = lax.all_gather(gram, ("dp", "tensor"), axis=0, tiled=True)
    gram = jnp.concatenate([gram[:rank], gram[rank:]], axis=1)
    inverse = inverse_factor(gram)

    coeff = jnp.concatenate([transposed_dot(summed, gate_rows), transposed_dot(summed, up_rows)], axis=1)
    coeff = sum_over(coeff.astype(jnp.bfloat16), "tensor").astype(jnp.bfloat16)
    coeff = lax.all_gather(coeff, ("dp", "tensor"), axis=0, tiled=True)
    down_rows = lax.all_gather(down_weight[0], "dp", axis=0, tiled=False)

    tok_rows = tokens.shape[0]
    top_count = routes.shape[1]
    capacity = tok_rows * top_count * 3 // (2 * experts)
    targets = routes.reshape(-1)
    assignments = targets.shape[0]
    onehot = (targets[:, None] == jnp.arange(experts, dtype=jnp.int32)[None, :]).astype(jnp.int32)
    place = jnp.sum((jnp.cumsum(onehot, axis=0) - 1) * onehot, axis=1)
    slot_index = targets * capacity + place
    owners = jnp.full((experts * capacity,), tok_rows, jnp.int32)
    owners = owners.at[slot_index].set(jnp.arange(assignments, dtype=jnp.int32) // top_count)
    padded = jnp.concatenate([tokens, jnp.zeros((1, tokens.shape[1]), tokens.dtype)], axis=0)
    outgoing = padded[owners].reshape(experts, capacity, tokens.shape[1])
    arrived = lax.all_to_all(outgoing, "expert", split_axis=0, concat_axis=0, tiled=True)
    arrived_rows = arrived.reshape(experts * capacity, tokens.shape[1])

    raw = jnp.dot(arrived_rows, summed, preferred_element_type=jnp.float32).astype(jnp.bfloat16)
    raw = sum_over(raw, "tensor").astype(jnp.bfloat16)
    raw = lax.all_gather(raw, "tensor", axis=0, tiled=True)

    projected = split_dot(inverse, raw, True).astype(jnp.bfloat16)
    answers = 0.0
    for index in range(2):
        block = split_dot(inverse, coeff[index * rank:(index + 1) * rank], False).astype(jnp.bfloat16)
        hidden_half = block.shape[1] // 2
        gate_part = jnp.dot(projected, block[:, :hidden_half], preferred_element_type=jnp.float32)
        up_part = jnp.dot(projected, block[:, hidden_half:], preferred_element_type=jnp.float32)
        hidden = (jax.nn.silu(gate_part) * up_part).astype(jnp.bfloat16)
        answers = answers + jnp.dot(hidden, down_rows[index], preferred_element_type=jnp.float32)
    answers = answers.astype(jnp.bfloat16)
    returned = lax.all_to_all(
        answers.reshape(experts, capacity, tokens.shape[1]),
        "expert",
        split_axis=0,
        concat_axis=0,
        tiled=True,
    )
    picked = returned.reshape(experts * capacity, tokens.shape[1])[slot_index].astype(jnp.float32)
    weighted = picked * route_weights.reshape(-1)[:, None]
    return jnp.sum(weighted.reshape(tok_rows, top_count, tokens.shape[1]), axis=1).astype(
        jnp.bfloat16
    )


def solution(mesh):
    return jax.shard_map(
        on_device,
        mesh=mesh,
        in_specs=(
            P(("expert", "dp"), "tensor"),
            P("expert", "tensor", "dp"),
            P("expert", "tensor", "dp"),
            P("expert", "dp", "tensor"),
            P("expert", None, "dp", None),
            P(),
            P(("expert", "dp"), None),
            P(("expert", "dp"), None),
        ),
        out_specs=P(("expert", "dp"), "tensor"),
        check_vma=False,
    )
```

```python
import jax
import jax.numpy as jnp
from jax import lax
from jax.experimental import pallas as pl
from jax.experimental.pallas import tpu as pltpu
from jax.sharding import PartitionSpec as P

MESH = pl.DeviceIdType.MESH
HIGHEST = lax.Precision.HIGHEST
BLK = 128


def factor_block(tiles, serve):
    lane = lax.broadcasted_iota(jnp.int32, (8, BLK), 1)
    sub = lax.broadcasted_iota(jnp.int32, (8, BLK), 0)
    n = BLK // 8
    tiles = list(tiles)
    for k in range(0, BLK, 2):
        t, r = divmod(k, 8)
        cur = tiles[t]
        col1 = jnp.broadcast_to(cur[:, k:k + 1], (8, BLK))
        col2 = jnp.broadcast_to(cur[:, k + 1:k + 2], (8, BLK))
        a = col1[r:r + 1, :]
        b = col1[r + 1:r + 2, :]
        c = col2[r + 1:r + 2, :]
        ra = 1.0 / a
        rc = a / (a * c - b * b)
        first, second = lane == k, lane == k + 1
        both = jnp.logical_or(first, second)
        row1 = jnp.where(first[:1], 1.0, jnp.where(second[:1], 0.0, cur[r:r + 1, :]))
        row2 = jnp.where(both[:1], 0.0, cur[r + 1:r + 2, :]) - (b * ra) * row1
        row2 = jnp.where(second[:1], 1.0, row2)
        v2 = rc * row2
        v1 = ra * row1 - (b * ra) * v2
        for i in range(t, n):
            old = tiles[i]
            if i == t:
                new = jnp.where(both, 0.0, old) - col1 * v1 - col2 * v2
                new = jnp.where(sub > r + 1, new, old)
                new = jnp.where(sub == r, row1 * jnp.sqrt(ra), new)
                new = jnp.where(sub == r + 1, row2 * jnp.sqrt(rc), new)
            else:
                c1 = jnp.broadcast_to(old[:, k:k + 1], (8, BLK))
                c2 = jnp.broadcast_to(old[:, k + 1:k + 2], (8, BLK))
                new = jnp.where(both, 0.0, old) - c1 * v1 - c2 * v2
            tiles[i] = new
        if k % 32 == 30:
            serve(k // 32)
    return [jnp.where(lane <= sub + 8 * i, tiles[i], 0.0) for i in range(n)]

def eliminate(out_ref, inv_ref, serve):
    size = out_ref.shape[0]
    steps = size // BLK

    def step(j, carry):
        at = pl.multiple_of(j * BLK, BLK)
        tiles = [out_ref[pl.ds(pl.multiple_of(at + 8 * i, 8), 8), pl.ds(at, BLK)] for i in range(BLK // 8)]
        for i, tile in enumerate(factor_block(tiles, lambda turn: serve(4 * j + turn))):
            inv_ref[8 * i:8 * i + 8, :] = tile
        inv = inv_ref[...]
        rows = lax.broadcasted_iota(jnp.int32, (BLK, BLK), 0)
        cols = lax.broadcasted_iota(jnp.int32, (BLK, BLK), 1)
        eye = jnp.where(rows == cols, 1.0, 0.0)
        out_ref[pl.ds(at, BLK), pl.ds(at, BLK)] = eye
        full = jnp.dot(inv, out_ref[pl.ds(at, BLK), :], precision=HIGHEST, preferred_element_type=jnp.float32)
        column = lax.broadcasted_iota(jnp.int32, (BLK, size), 1)
        later = jnp.where(column >= at + BLK, full, 0.0)
        out_ref[pl.ds(at, BLK), :] = full
        column = lax.broadcasted_iota(jnp.int32, (size, size), 1)
        row = lax.broadcasted_iota(jnp.int32, (size, size), 0)
        zero = (column >= at) & (column < at + BLK) & (row >= at + BLK)
        out_ref[...] = jnp.where(zero, 0.0, out_ref[...]) - lax.dot_general(
            later, full, (((0,), (0,)), ((), ())), precision=HIGHEST, preferred_element_type=jnp.float32)
        return carry

    lax.fori_loop(0, steps, step, 0)
    row = lax.broadcasted_iota(jnp.int32, (size, size), 0)
    column = lax.broadcasted_iota(jnp.int32, (size, size), 1)
    out_ref[...] = jnp.where(column <= row, out_ref[...], 0.0)

REACH = 3
CUTS = 4


def cluster_kernel(part_ref, weight_ref, out_ref, stage, got, own, plus, minus, acc,
                   dp_send, dp_recv, up_send, up_recv, low_send, low_recv, fin_send, fin_recv):
    count = lax.axis_size("expert")
    me = lax.axis_index("expert")
    half = lax.axis_index("dp")
    sibling = {"dp": 1 - half}
    after = {"expert": lax.rem(me + 1, count)}
    before = {"expert": lax.rem(me + count - 1, count)}
    part = part_ref.shape[0] // 2
    size = part // CUTS
    barrier = pltpu.get_barrier_semaphore()
    for device in (sibling, after, before):
        pl.semaphore_signal(barrier, inc=1, device_id=device, device_id_type=MESH)

    def rows(side, cut):
        return pl.ds(pl.multiple_of(side * part + cut * size, 16), size)

    def remote(src, dst, send, recv, device):
        return pltpu.make_async_remote_copy(
            src_ref=src, dst_ref=dst, send_sem=send, recv_sem=recv, device_id=device, device_id_type=MESH)

    def swap(cut):
        return remote(stage.at[cut], got.at[cut], dp_send.at[cut], dp_recv.at[cut], sibling)

    def ahead(hop, cut):
        source = own.at[cut] if hop == 0 else plus.at[hop - 1, cut]
        return remote(source, plus.at[hop, cut], up_send.at[hop, cut], up_recv.at[hop, cut], after)

    def back(hop, cut):
        source = own.at[cut] if hop == 0 else minus.at[hop - 1, cut]
        return remote(source, minus.at[hop, cut], low_send.at[hop, cut], low_recv.at[hop, cut], before)

    def finish(cut):
        place = out_ref.at[rows(half, cut)]
        return remote(place, place, fin_send.at[cut], fin_recv.at[cut], sibling)

    for cut in range(CUTS):
        stage[cut] = part_ref[rows(1 - half, cut), :].astype(jnp.bfloat16)
    pl.semaphore_wait(barrier, 3)
    for cut in range(CUTS):
        swap(cut).start()
    for cut in range(CUTS):
        swap(cut).wait_recv()
        value = (part_ref[rows(half, cut), :] + got[cut].astype(jnp.float32)).astype(jnp.bfloat16)
        own[cut] = value
        ahead(0, cut).start()
        back(0, cut).start()
        acc[cut] = value.astype(jnp.float32)
    for hop in range(REACH):
        for cut in range(CUTS):
            ahead(hop, cut).wait_recv()
            if hop < REACH - 1:
                ahead(hop + 1, cut).start()
            back(hop, cut).wait_recv()
            if hop < REACH - 1:
                back(hop + 1, cut).start()
            total = acc[cut] + weight_ref[hop:hop + 1, :] * plus[hop, cut].astype(jnp.float32)
            total = total + weight_ref[REACH + hop:REACH + hop + 1, :] * minus[hop, cut].astype(jnp.float32)
            if hop < REACH - 1:
                acc[cut] = total
            else:
                out_ref[rows(half, cut), :] = total.astype(jnp.bfloat16)
                finish(cut).start()
    for cut in range(CUTS):
        finish(cut).wait_recv()
        finish(cut).wait_send()
        swap(cut).wait_send()
        for hop in range(REACH):
            ahead(hop, cut).wait_send()
            back(hop, cut).wait_send()


def cluster_sum(sketched, weights):
    rows, rank = sketched.shape
    size = rows // 2 // CUTS
    return pl.pallas_call(
        cluster_kernel,
        out_shape=jax.ShapeDtypeStruct((rows, rank), jnp.bfloat16),
        in_specs=[pl.BlockSpec(memory_space=pltpu.VMEM)] * 2,
        out_specs=pl.BlockSpec(memory_space=pltpu.VMEM),
        scratch_shapes=[
            pltpu.VMEM((CUTS, size, rank), jnp.bfloat16),
            pltpu.VMEM((CUTS, size, rank), jnp.bfloat16),
            pltpu.VMEM((CUTS, size, rank), jnp.bfloat16),
            pltpu.VMEM((REACH, CUTS, size, rank), jnp.bfloat16),
            pltpu.VMEM((REACH, CUTS, size, rank), jnp.bfloat16),
            pltpu.VMEM((CUTS, size, rank), jnp.float32),
            pltpu.SemaphoreType.DMA((CUTS,)),
            pltpu.SemaphoreType.DMA((CUTS,)),
            pltpu.SemaphoreType.DMA((REACH, CUTS)),
            pltpu.SemaphoreType.DMA((REACH, CUTS)),
            pltpu.SemaphoreType.DMA((REACH, CUTS)),
            pltpu.SemaphoreType.DMA((REACH, CUTS)),
            pltpu.SemaphoreType.DMA((CUTS,)),
            pltpu.SemaphoreType.DMA((CUTS,)),
        ],
        compiler_params=pltpu.CompilerParams(collective_id=3, has_side_effects=True),
        cost_estimate=pl.CostEstimate(flops=10 ** 10, bytes_accessed=8 * rows * rank, transcendentals=0),
    )(sketched, weights)


def gram_kernel(part_ref, down_ref, out_ref, other_ref, arrive, pieces, rs_send, rs_recv, ag_send, ag_recv, sib_send, sib_recv, down_send, down_recv):
    me = lax.axis_index("tensor")
    half = lax.axis_index("dp")
    count = part_ref.shape[0]
    height, width = part_ref.shape[1:]
    sibling = {"dp": 1 - half}
    barrier = pltpu.get_barrier_semaphore()
    for step in range(1, count):
        pl.semaphore_signal(barrier, inc=1, device_id={"tensor": lax.rem(me + step, count)}, device_id_type=MESH)
    pl.semaphore_signal(barrier, inc=1, device_id=sibling, device_id_type=MESH)
    pl.semaphore_wait(barrier, count)

    def scatter(step):
        peer = lax.rem(me + step, count)
        return pltpu.make_async_remote_copy(
            src_ref=part_ref.at[peer], dst_ref=arrive.at[step], send_sem=rs_send.at[step], recv_sem=rs_recv.at[step],
            device_id={"tensor": peer}, device_id_type=MESH)

    def spread(step):
        peer = lax.rem(me + step, count)
        mine = half * count + me
        return pltpu.make_async_remote_copy(
            src_ref=pieces.at[mine], dst_ref=pieces.at[mine], send_sem=ag_send.at[step], recv_sem=ag_recv.at[step],
            device_id={"tensor": peer}, device_id_type=MESH)

    def hand(step):
        piece = half * count + lax.rem(me + count - step, count)
        return pltpu.make_async_remote_copy(
            src_ref=pieces.at[piece], dst_ref=pieces.at[piece], send_sem=sib_send.at[step], recv_sem=sib_recv.at[step],
            device_id=sibling, device_id_type=MESH)

    down = pltpu.make_async_remote_copy(
        src_ref=down_ref, dst_ref=other_ref, send_sem=down_send, recv_sem=down_recv,
        device_id=sibling, device_id_type=MESH)
    order = [4, 3, 5, 2, 6, 1, 7]
    for step in order:
        scatter(step).start()
    down.start()
    total = part_ref[me]
    for step in reversed(order):
        scatter(step).wait_recv()
        total = total + arrive[step]
    pieces[half * count + me] = total
    for step in order:
        spread(step).start()
    hand(0).start()
    for step in reversed(order):
        spread(step).wait_recv()
        hand(step).start()
    for step in range(count):
        hand(step).wait_recv()
    for side in range(2):
        for piece in range(count):
            out_ref[piece * height:(piece + 1) * height, side * width:(side + 1) * width] = pieces[side * count + piece]
    for step in order:
        scatter(step).wait_send()
        spread(step).wait_send()
    for step in range(count):
        hand(step).wait_send()
    down.wait()


def gram_sum(part, down):
    count, height, width = part.shape
    size = count * height
    return pl.pallas_call(
        gram_kernel,
        out_shape=[jax.ShapeDtypeStruct((size, size), jnp.float32), jax.ShapeDtypeStruct(down.shape, down.dtype)],
        in_specs=[pl.BlockSpec(memory_space=pltpu.VMEM), pl.BlockSpec(memory_space=pl.ANY)],
        out_specs=[pl.BlockSpec(memory_space=pltpu.VMEM), pl.BlockSpec(memory_space=pl.ANY)],
        scratch_shapes=[
            pltpu.VMEM((count, height, width), jnp.float32),
            pltpu.VMEM((2 * count, height, width), jnp.float32),
        ] + [pltpu.SemaphoreType.DMA((count,))] * 6 + [pltpu.SemaphoreType.DMA] * 2,
        compiler_params=pltpu.CompilerParams(collective_id=1, has_side_effects=True),
        cost_estimate=pl.CostEstimate(flops=40 * 10 ** 9, bytes_accessed=8 * size * size, transcendentals=0),
    )(part, down)


def factor_kernel(gram_ref, coeff_ref, raw_ref, out_ref, coeff_all, raw_all, inv_ref, coeff_slot, raw_slot,
                  send, recv, sib_send, sib_recv):
    count = coeff_ref.shape[1]
    hops = count - 1
    me = lax.axis_index("tensor")
    half = lax.axis_index("dp")
    sibling = {"dp": 1 - half}
    neighbours = ({"tensor": lax.rem(me + 1, count)}, {"tensor": lax.rem(me + hops, count)})
    barrier = pltpu.get_barrier_semaphore()
    for device in (sibling,) + neighbours:
        pl.semaphore_signal(barrier, inc=1, device_id=device, device_id_type=MESH)
    pl.semaphore_wait(barrier, 3)

    def chunk(side, distance):
        return lax.rem(me + (2 * count - distance if side == 0 else distance), count)

    def place(kind, side, index):
        return coeff_all.at[0, side, index] if kind == 0 else raw_all.at[side, index]

    def remote(src, dst, kind, side, turn):
        return pltpu.make_async_remote_copy(
            src_ref=src, dst_ref=dst, send_sem=send.at[kind, side, turn], recv_sem=recv.at[kind, side, turn],
            device_id=neighbours[side], device_id_type=MESH)

    def first(kind, side):
        part = (coeff_ref, raw_ref)[kind].at[side, chunk(side, 1)]
        return remote(part, (coeff_slot, raw_slot)[kind].at[side, 0], kind, side, 0)

    def add_on(kind, side, turn):
        slot = (coeff_slot, raw_slot)[kind]
        return remote(slot.at[side, turn - 1], slot.at[side, turn], kind, side, turn)

    def pass_on(kind, side, turn):
        here = place(kind, side, chunk(side, turn - hops))
        return remote(here, here, kind, side, turn)

    def share(side, number):
        index = chunk(side, number)
        return pltpu.make_async_remote_copy(
            src_ref=coeff_all.at[0, side, index], dst_ref=coeff_all.at[1, side, index],
            send_sem=sib_send.at[side, number], recv_sem=sib_recv.at[side, number],
            device_id=sibling, device_id_type=MESH)

    both = [(kind, side) for kind in range(2) for side in range(2)]
    for kind, side in both:
        first(kind, side).start()

    def serve(turn):
        @pl.when(turn < hops)
        def _():
            for kind, side in both:
                slot = (coeff_slot, raw_slot)[kind]
                remote(slot.at[side, turn], slot.at[side, turn], kind, side, turn).wait_recv()
                part = (coeff_ref, raw_ref)[kind][side, chunk(side, turn + 2)]
                value = (slot[side, turn].astype(jnp.float32) + part.astype(jnp.float32)).astype(jnp.bfloat16)

                @pl.when(turn < hops - 1)
                def _():
                    slot[side, turn] = value
                    add_on(kind, side, turn + 1).start()

                @pl.when(turn == hops - 1)
                def _():
                    place(kind, side, me)[...] = value
                    pass_on(kind, side, turn + 1).start()
                    if kind == 0:
                        share(side, 0).start()

        @pl.when((turn >= hops) & (turn < 2 * hops))
        def _():
            for kind, side in both:
                here = place(kind, side, chunk(side, turn - hops + 1))
                remote(here, here, kind, side, turn).wait_recv()

                @pl.when(turn < 2 * hops - 1)
                def _():
                    pass_on(kind, side, turn + 1).start()

                if kind == 0:
                    share(side, turn - hops + 1).start()

    out_ref[...] = gram_ref[...]
    eliminate(out_ref, inv_ref, serve)

    for kind, side in both:
        first(kind, side).wait_send()

    def drain(turn, carry):
        for kind, side in both:
            @pl.when(turn < hops)
            def _():
                add_on(kind, side, turn).wait_send()

            @pl.when(turn >= hops)
            def _():
                pass_on(kind, side, turn).wait_send()
        return carry

    lax.fori_loop(1, 2 * hops, drain, 0)

    def shared(number, carry):
        for side in range(2):
            share(side, number).wait_send()
            share(side, number).wait_recv()
        return carry

    lax.fori_loop(0, count, shared, 0)


def inverse_and_sums(gram, coeff, raw):
    size = gram.shape[0]
    count = coeff.shape[1]
    steps = 2 * (count - 1)
    slots = lambda array: (2, count - 1) + array.shape[2:]
    return pl.pallas_call(
        factor_kernel,
        out_shape=[
            jax.ShapeDtypeStruct((size, size), jnp.float32),
            jax.ShapeDtypeStruct((2,) + coeff.shape, jnp.bfloat16),
            jax.ShapeDtypeStruct(raw.shape, jnp.bfloat16),
        ],
        in_specs=[pl.BlockSpec(memory_space=pltpu.VMEM)] * 3,
        out_specs=[pl.BlockSpec(memory_space=pltpu.VMEM)] * 3,
        scratch_shapes=[
            pltpu.VMEM((BLK, BLK), jnp.float32),
            pltpu.VMEM(slots(coeff), jnp.bfloat16),
            pltpu.VMEM(slots(raw), jnp.bfloat16),
            pltpu.SemaphoreType.DMA((2, 2, steps)),
            pltpu.SemaphoreType.DMA((2, 2, steps)),
            pltpu.SemaphoreType.DMA((2, count)),
            pltpu.SemaphoreType.DMA((2, count)),
        ],
        compiler_params=pltpu.CompilerParams(collective_id=2, has_side_effects=True),
        cost_estimate=pl.CostEstimate(flops=40 * 10 ** 9, bytes_accessed=8 * size * size, transcendentals=0),
    )(gram, coeff, raw)


def split_dot(precise, plain, transposed):
    high = precise.astype(jnp.bfloat16)
    low = (precise - high.astype(jnp.float32)).astype(jnp.bfloat16)
    if transposed:
        dims = (((1,), (1,)), ((), ()))
        return lax.dot_general(plain, high, dims, preferred_element_type=jnp.float32) + lax.dot_general(
            plain, low, dims, preferred_element_type=jnp.float32)
    dims = (((1,), (0,)), ((), ()))
    return lax.dot_general(high, plain, dims, preferred_element_type=jnp.float32) + lax.dot_general(
        low, plain, dims, preferred_element_type=jnp.float32)


def transposed_dot(left, right):
    return lax.dot_general(left, right, (((0,), (0,)), ((), ())), preferred_element_type=jnp.float32)


def on_device(tokens, gate_weight, up_weight, down_weight, sketch, clusters, routes, route_weights):
    gate_rows = gate_weight[0]
    up_rows = up_weight[0]
    experts = lax.axis_size("expert")
    tensors = lax.axis_size("tensor")
    half = lax.axis_index("dp")
    position = lax.axis_index("expert")
    sketched = jnp.dot(gate_rows, sketch[0, 0], preferred_element_type=jnp.float32) + jnp.dot(
        up_rows, sketch[0, 1], preferred_element_type=jnp.float32
    )
    rank = sketched.shape[1]

    offsets = jnp.array([-1, -2, -3, 1, 2, 3, 0, 0], jnp.int32)
    others = position + offsets
    inside = (others >= 0) & (others < experts)
    same = inside & (clusters[jnp.clip(others, 0, experts - 1)] == clusters[position])
    weights = jnp.broadcast_to(same.astype(jnp.float32)[:, None], (8, rank))
    summed = cluster_sum(sketched, weights)

    tok_rows, width = tokens.shape
    top_count = routes.shape[1]
    capacity = tok_rows * top_count * 3 // (2 * experts)
    named = routes.T[None] == jnp.arange(experts, dtype=jnp.int32)[:, None, None]
    chosen = jnp.any(named, axis=1)
    shares = jnp.sum(jnp.where(named, route_weights.T[None], 0.0), axis=1)
    token_index = jnp.arange(tok_rows)
    earlier = (token_index[:, None] < token_index[None, :]).astype(jnp.bfloat16)
    place = jnp.dot(chosen.astype(jnp.bfloat16), earlier, preferred_element_type=jnp.float32).astype(jnp.int32)
    holds = chosen[:, None, :] & (place[:, None, :] == jnp.arange(capacity, dtype=jnp.int32)[None, :, None])
    select = holds.astype(jnp.bfloat16).reshape(experts * capacity, tok_rows)
    outgoing = jnp.dot(select, tokens, preferred_element_type=jnp.float32).astype(jnp.bfloat16)
    outgoing = outgoing.reshape(experts, capacity, width)

    columns = lax.dynamic_slice_in_dim(summed, half * (rank // 2), rank // 2, 1)
    gram = transposed_dot(summed, columns).reshape(tensors, rank // tensors, rank // 2)
    coeff = jnp.stack([transposed_dot(summed, gate_rows), transposed_dot(summed, up_rows)]).astype(jnp.bfloat16)
    coeff = coeff.reshape(2, tensors, rank // tensors, coeff.shape[2])
    gram, outgoing, coeff = lax.optimization_barrier((gram, outgoing, coeff))
    arrived = lax.all_to_all(outgoing, "expert", split_axis=0, concat_axis=0, tiled=True)
    gram, down_other = gram_sum(gram, down_weight[0])
    arrived, gram = lax.optimization_barrier((arrived, gram))
    raw = jnp.dot(arrived.reshape(experts * capacity, width), summed, preferred_element_type=jnp.float32)
    raw = raw.astype(jnp.bfloat16).reshape(2, tensors, experts * capacity // (2 * tensors), rank)
    inverse, coeff, raw = inverse_and_sums(gram, coeff, raw)

    projected = split_dot(inverse, raw.reshape(experts * capacity, rank), True).astype(jnp.bfloat16)
    answers = 0.0
    for index, down_rows in enumerate((down_weight[0], down_other)):
        gate_coeff = split_dot(inverse, coeff[index, 0].reshape(rank, -1), False).astype(jnp.bfloat16)
        up_coeff = split_dot(inverse, coeff[index, 1].reshape(rank, -1), False).astype(jnp.bfloat16)
        gate_part = jnp.dot(projected, gate_coeff, preferred_element_type=jnp.float32)
        up_part = jnp.dot(projected, up_coeff, preferred_element_type=jnp.float32)
        hidden = (jax.nn.silu(gate_part) * up_part).astype(jnp.bfloat16)
        answers = answers + jnp.dot(hidden, down_rows, preferred_element_type=jnp.float32)
    answers = answers.astype(jnp.bfloat16).reshape(experts, capacity, width)
    returned = lax.all_to_all(answers, "expert", split_axis=0, concat_axis=0, tiled=True)
    returned = returned.reshape(experts * capacity, width)
    mixing = jnp.where(holds, shares[:, None, :], 0.0).reshape(experts * capacity, tok_rows)
    high = mixing.astype(jnp.bfloat16)
    low = (mixing - high.astype(jnp.float32)).astype(jnp.bfloat16)
    return (transposed_dot(high, returned) + transposed_dot(low, returned)).astype(jnp.bfloat16)


def solution(mesh):
    return jax.shard_map(
        on_device,
        mesh=mesh,
        in_specs=(
            P(("expert", "dp"), "tensor"),
            P("expert", "tensor", "dp"),
            P("expert", "tensor", "dp"),
            P("expert", "dp", "tensor"),
            P("expert", None, "dp", None),
            P(),
            P(("expert", "dp"), None),
            P(("expert", "dp"), None),
        ),
        out_specs=P(("expert", "dp"), "tensor"),
        check_vma=False,
    )
```

```python
import jax
import jax.numpy as jnp
from jax import lax
from jax.experimental import pallas as pl
from jax.experimental.pallas import tpu as pltpu
from jax.sharding import PartitionSpec as P

MESH = pl.DeviceIdType.MESH
HIGHEST = lax.Precision.HIGHEST
BLK = 128


def factor_block(tiles, serve):
    lane = lax.broadcasted_iota(jnp.int32, (8, BLK), 1)
    sub = lax.broadcasted_iota(jnp.int32, (8, BLK), 0)
    n = BLK // 8
    tiles = list(tiles)
    for k in range(0, BLK, 2):
        t, r = divmod(k, 8)
        cur = tiles[t]
        col1 = jnp.broadcast_to(cur[:, k:k + 1], (8, BLK))
        col2 = jnp.broadcast_to(cur[:, k + 1:k + 2], (8, BLK))
        a = col1[r:r + 1, :]
        b = col1[r + 1:r + 2, :]
        c = col2[r + 1:r + 2, :]
        ra = 1.0 / a
        rc = a / (a * c - b * b)
        first, second = lane == k, lane == k + 1
        both = jnp.logical_or(first, second)
        row1 = jnp.where(first[:1], 1.0, jnp.where(second[:1], 0.0, cur[r:r + 1, :]))
        row2 = jnp.where(both[:1], 0.0, cur[r + 1:r + 2, :]) - (b * ra) * row1
        row2 = jnp.where(second[:1], 1.0, row2)
        v2 = rc * row2
        v1 = ra * row1 - (b * ra) * v2
        for i in range(t, n):
            old = tiles[i]
            if i == t:
                new = jnp.where(both, 0.0, old) - col1 * v1 - col2 * v2
                new = jnp.where(sub > r + 1, new, old)
                new = jnp.where(sub == r, row1 * jnp.sqrt(ra), new)
                new = jnp.where(sub == r + 1, row2 * jnp.sqrt(rc), new)
            else:
                c1 = jnp.broadcast_to(old[:, k:k + 1], (8, BLK))
                c2 = jnp.broadcast_to(old[:, k + 1:k + 2], (8, BLK))
                new = jnp.where(both, 0.0, old) - c1 * v1 - c2 * v2
            tiles[i] = new
        if k % 16 == 14:
            serve(k // 16)
    return [jnp.where(lane <= sub + 8 * i, tiles[i], 0.0) for i in range(n)]

def eliminate(out_ref, inv_ref, serve):
    size = out_ref.shape[0]
    steps = size // BLK

    def step(j, carry):
        at = pl.multiple_of(j * BLK, BLK)
        tiles = [out_ref[pl.ds(pl.multiple_of(at + 8 * i, 8), 8), pl.ds(at, BLK)] for i in range(BLK // 8)]
        for i, tile in enumerate(factor_block(tiles, lambda turn: serve(turn % 2, 4 * j + turn // 2))):
            inv_ref[8 * i:8 * i + 8, :] = tile
        inv = inv_ref[...]
        rows = lax.broadcasted_iota(jnp.int32, (BLK, BLK), 0)
        cols = lax.broadcasted_iota(jnp.int32, (BLK, BLK), 1)
        eye = jnp.where(rows == cols, 1.0, 0.0)
        out_ref[pl.ds(at, BLK), pl.ds(at, BLK)] = eye
        full = jnp.dot(inv, out_ref[pl.ds(at, BLK), :], precision=HIGHEST, preferred_element_type=jnp.float32)
        column = lax.broadcasted_iota(jnp.int32, (BLK, size), 1)
        later = jnp.where(column >= at + BLK, full, 0.0)
        out_ref[pl.ds(at, BLK), :] = full
        column = lax.broadcasted_iota(jnp.int32, (size, size), 1)
        row = lax.broadcasted_iota(jnp.int32, (size, size), 0)
        zero = (column >= at) & (column < at + BLK) & (row >= at + BLK)
        out_ref[...] = jnp.where(zero, 0.0, out_ref[...]) - lax.dot_general(
            later, full, (((0,), (0,)), ((), ())), precision=HIGHEST, preferred_element_type=jnp.float32)
        return carry

    lax.fori_loop(0, steps, step, 0)
    row = lax.broadcasted_iota(jnp.int32, (size, size), 0)
    column = lax.broadcasted_iota(jnp.int32, (size, size), 1)
    out_ref[...] = jnp.where(column <= row, out_ref[...], 0.0)

REACH = 3
CUTS = 4


def cluster_kernel(part_ref, cluster_ref, out_ref, stage, got, own, plus, minus, acc,
                   dp_send, dp_recv, up_send, up_recv, low_send, low_recv, fin_send, fin_recv):
    count = lax.axis_size("expert")
    me = lax.axis_index("expert")
    half = lax.axis_index("dp")
    sibling = {"dp": 1 - half}
    after = {"expert": lax.rem(me + 1, count)}
    before = {"expert": lax.rem(me + count - 1, count)}
    part = part_ref.shape[0] // 2
    size = part // CUTS
    mine = cluster_ref[me]

    def share(step):
        other = me + step
        inside = jnp.logical_and(other >= 0, other < count)
        same = cluster_ref[lax.rem(other + count, count)] == mine
        return jnp.where(jnp.logical_and(inside, same), 1.0, 0.0).astype(jnp.float32)

    barrier = pltpu.get_barrier_semaphore()
    for device in (sibling, after, before):
        pl.semaphore_signal(barrier, inc=1, device_id=device, device_id_type=MESH)

    def rows(side, cut):
        return pl.ds(pl.multiple_of(side * part + cut * size, 16), size)

    def remote(src, dst, send, recv, device):
        return pltpu.make_async_remote_copy(
            src_ref=src, dst_ref=dst, send_sem=send, recv_sem=recv, device_id=device, device_id_type=MESH)

    def swap(cut):
        return remote(stage.at[cut], got.at[cut], dp_send.at[cut], dp_recv.at[cut], sibling)

    def ahead(hop, cut):
        source = own.at[cut] if hop == 0 else plus.at[hop - 1, cut]
        return remote(source, plus.at[hop, cut], up_send.at[hop, cut], up_recv.at[hop, cut], after)

    def back(hop, cut):
        source = own.at[cut] if hop == 0 else minus.at[hop - 1, cut]
        return remote(source, minus.at[hop, cut], low_send.at[hop, cut], low_recv.at[hop, cut], before)

    def finish(cut):
        place = out_ref.at[rows(half, cut)]
        return remote(place, place, fin_send.at[cut], fin_recv.at[cut], sibling)

    for cut in range(CUTS):
        stage[cut] = part_ref[rows(1 - half, cut), :].astype(jnp.bfloat16)
    pl.semaphore_wait(barrier, 3)
    for cut in range(CUTS):
        swap(cut).start()
    for cut in range(CUTS):
        swap(cut).wait_recv()
        value = (part_ref[rows(half, cut), :] + got[cut].astype(jnp.float32)).astype(jnp.bfloat16)
        own[cut] = value
        ahead(0, cut).start()
        back(0, cut).start()
        acc[cut] = value.astype(jnp.float32)
    for hop in range(REACH):
        for cut in range(CUTS):
            ahead(hop, cut).wait_recv()
            if hop < REACH - 1:
                ahead(hop + 1, cut).start()
            back(hop, cut).wait_recv()
            if hop < REACH - 1:
                back(hop + 1, cut).start()
            total = acc[cut] + share(-1 - hop) * plus[hop, cut].astype(jnp.float32)
            total = total + share(hop + 1) * minus[hop, cut].astype(jnp.float32)
            if hop < REACH - 1:
                acc[cut] = total
            else:
                out_ref[rows(half, cut), :] = total.astype(jnp.bfloat16)
                finish(cut).start()
    for cut in range(CUTS):
        finish(cut).wait_recv()
        finish(cut).wait_send()
        swap(cut).wait_send()
        for hop in range(REACH):
            ahead(hop, cut).wait_send()
            back(hop, cut).wait_send()


def cluster_sum(sketched, clusters):
    rows, rank = sketched.shape
    size = rows // 2 // CUTS
    return pl.pallas_call(
        cluster_kernel,
        out_shape=jax.ShapeDtypeStruct((rows, rank), jnp.bfloat16),
        in_specs=[pl.BlockSpec(memory_space=pltpu.VMEM), pl.BlockSpec(memory_space=pltpu.SMEM)],
        out_specs=pl.BlockSpec(memory_space=pltpu.VMEM),
        scratch_shapes=[
            pltpu.VMEM((CUTS, size, rank), jnp.bfloat16),
            pltpu.VMEM((CUTS, size, rank), jnp.bfloat16),
            pltpu.VMEM((CUTS, size, rank), jnp.bfloat16),
            pltpu.VMEM((REACH, CUTS, size, rank), jnp.bfloat16),
            pltpu.VMEM((REACH, CUTS, size, rank), jnp.bfloat16),
            pltpu.VMEM((CUTS, size, rank), jnp.float32),
            pltpu.SemaphoreType.DMA((CUTS,)),
            pltpu.SemaphoreType.DMA((CUTS,)),
            pltpu.SemaphoreType.DMA((REACH, CUTS)),
            pltpu.SemaphoreType.DMA((REACH, CUTS)),
            pltpu.SemaphoreType.DMA((REACH, CUTS)),
            pltpu.SemaphoreType.DMA((REACH, CUTS)),
            pltpu.SemaphoreType.DMA((CUTS,)),
            pltpu.SemaphoreType.DMA((CUTS,)),
        ],
        compiler_params=pltpu.CompilerParams(collective_id=3, has_side_effects=True),
        cost_estimate=pl.CostEstimate(flops=10 ** 10, bytes_accessed=8 * rows * rank, transcendentals=0),
    )(sketched, clusters)


def gram_kernel(part_ref, down_ref, out_ref, other_ref, arrive, pieces, rs_send, rs_recv, ag_send, ag_recv, sib_send, sib_recv, down_send, down_recv):
    me = lax.axis_index("tensor")
    half = lax.axis_index("dp")
    count = part_ref.shape[0]
    height, width = part_ref.shape[1:]
    sibling = {"dp": 1 - half}
    barrier = pltpu.get_barrier_semaphore()
    for step in range(1, count):
        pl.semaphore_signal(barrier, inc=1, device_id={"tensor": lax.rem(me + step, count)}, device_id_type=MESH)
    pl.semaphore_signal(barrier, inc=1, device_id=sibling, device_id_type=MESH)
    pl.semaphore_wait(barrier, count)

    def scatter(step):
        peer = lax.rem(me + step, count)
        return pltpu.make_async_remote_copy(
            src_ref=part_ref.at[peer], dst_ref=arrive.at[step], send_sem=rs_send.at[step], recv_sem=rs_recv.at[step],
            device_id={"tensor": peer}, device_id_type=MESH)

    def spread(step):
        peer = lax.rem(me + step, count)
        mine = half * count + me
        return pltpu.make_async_remote_copy(
            src_ref=pieces.at[mine], dst_ref=pieces.at[mine], send_sem=ag_send.at[step], recv_sem=ag_recv.at[step],
            device_id={"tensor": peer}, device_id_type=MESH)

    def hand(step):
        piece = half * count + lax.rem(me + count - step, count)
        return pltpu.make_async_remote_copy(
            src_ref=pieces.at[piece], dst_ref=pieces.at[piece], send_sem=sib_send.at[step], recv_sem=sib_recv.at[step],
            device_id=sibling, device_id_type=MESH)

    down = pltpu.make_async_remote_copy(
        src_ref=down_ref, dst_ref=other_ref, send_sem=down_send, recv_sem=down_recv,
        device_id=sibling, device_id_type=MESH)
    order = [4, 3, 5, 2, 6, 1, 7]
    for step in order:
        scatter(step).start()
    down.start()
    total = part_ref[me]
    for step in reversed(order):
        scatter(step).wait_recv()
        total = total + arrive[step]
    pieces[half * count + me] = total
    for step in order:
        spread(step).start()
    hand(0).start()
    for step in reversed(order):
        spread(step).wait_recv()
        hand(step).start()
    for step in range(count):
        hand(step).wait_recv()
    for side in range(2):
        for piece in range(count):
            out_ref[piece * height:(piece + 1) * height, side * width:(side + 1) * width] = pieces[side * count + piece]
    for step in order:
        scatter(step).wait_send()
        spread(step).wait_send()
    for step in range(count):
        hand(step).wait_send()
    down.wait()


def gram_sum(part, down):
    count, height, width = part.shape
    size = count * height
    return pl.pallas_call(
        gram_kernel,
        out_shape=[jax.ShapeDtypeStruct((size, size), jnp.float32), jax.ShapeDtypeStruct(down.shape, down.dtype)],
        in_specs=[pl.BlockSpec(memory_space=pltpu.VMEM), pl.BlockSpec(memory_space=pl.ANY)],
        out_specs=[pl.BlockSpec(memory_space=pltpu.VMEM), pl.BlockSpec(memory_space=pl.ANY)],
        scratch_shapes=[
            pltpu.VMEM((count, height, width), jnp.float32),
            pltpu.VMEM((2 * count, height, width), jnp.float32),
        ] + [pltpu.SemaphoreType.DMA((count,))] * 6 + [pltpu.SemaphoreType.DMA] * 2,
        compiler_params=pltpu.CompilerParams(collective_id=1, has_side_effects=True),
        cost_estimate=pl.CostEstimate(flops=40 * 10 ** 9, bytes_accessed=8 * size * size, transcendentals=0),
    )(part, down)


def factor_kernel(gram_ref, coeff_ref, raw_ref, high_ref, low_ref, coeff_all, raw_all, out_ref, inv_ref, coeff_slot, raw_slot,
                  send, recv, sib_send, sib_recv):
    count = coeff_ref.shape[1]
    hops = count - 1
    me = lax.axis_index("tensor")
    half = lax.axis_index("dp")
    sibling = {"dp": 1 - half}
    neighbours = ({"tensor": lax.rem(me + 1, count)}, {"tensor": lax.rem(me + hops, count)})
    barrier = pltpu.get_barrier_semaphore()
    for device in (sibling,) + neighbours:
        pl.semaphore_signal(barrier, inc=1, device_id=device, device_id_type=MESH)
    pl.semaphore_wait(barrier, 3)

    def chunk(side, distance):
        return lax.rem(me + (2 * count - distance if side == 0 else distance), count)

    def place(kind, side, index):
        return coeff_all.at[0, side, index] if kind == 0 else raw_all.at[side, index]

    def remote(src, dst, kind, side, turn):
        return pltpu.make_async_remote_copy(
            src_ref=src, dst_ref=dst, send_sem=send.at[kind, side, turn], recv_sem=recv.at[kind, side, turn],
            device_id=neighbours[side], device_id_type=MESH)

    def first(kind, side):
        part = (coeff_ref, raw_ref)[kind].at[side, chunk(side, 1)]
        return remote(part, (coeff_slot, raw_slot)[kind].at[side, 0], kind, side, 0)

    def add_on(kind, side, turn):
        slot = (coeff_slot, raw_slot)[kind]
        return remote(slot.at[side, turn - 1], slot.at[side, turn], kind, side, turn)

    def pass_on(kind, side, turn):
        here = place(kind, side, chunk(side, turn - hops))
        return remote(here, here, kind, side, turn)

    def share(side, number):
        index = chunk(side, number)
        return pltpu.make_async_remote_copy(
            src_ref=coeff_all.at[0, side, index], dst_ref=coeff_all.at[1, side, index],
            send_sem=sib_send.at[side, number], recv_sem=sib_recv.at[side, number],
            device_id=sibling, device_id_type=MESH)

    both = [(kind, side) for kind in range(2) for side in range(2)]
    for kind, side in both:
        first(kind, side).start()

    def serve(kind, turn):
        @pl.when(turn < hops)
        def _():
            for side in range(2):
                slot = (coeff_slot, raw_slot)[kind]
                remote(slot.at[side, turn], slot.at[side, turn], kind, side, turn).wait_recv()
                part = (coeff_ref, raw_ref)[kind][side, chunk(side, turn + 2)]
                value = (slot[side, turn].astype(jnp.float32) + part.astype(jnp.float32)).astype(jnp.bfloat16)

                @pl.when(turn < hops - 1)
                def _():
                    slot[side, turn] = value
                    add_on(kind, side, turn + 1).start()

                @pl.when(turn == hops - 1)
                def _():
                    place(kind, side, me)[...] = value
                    pass_on(kind, side, turn + 1).start()
                    if kind == 0:
                        share(side, 0).start()

        @pl.when((turn >= hops) & (turn < 2 * hops))
        def _():
            for side in range(2):
                here = place(kind, side, chunk(side, turn - hops + 1))
                remote(here, here, kind, side, turn).wait_recv()

                @pl.when(turn < 2 * hops - 1)
                def _():
                    pass_on(kind, side, turn + 1).start()

                if kind == 0:
                    share(side, turn - hops + 1).start()

    out_ref[...] = gram_ref[...]
    eliminate(out_ref, inv_ref, serve)
    high = out_ref[...].astype(jnp.bfloat16)
    high_ref[...] = high
    low_ref[...] = (out_ref[...] - high.astype(jnp.float32)).astype(jnp.bfloat16)

    for kind, side in both:
        first(kind, side).wait_send()

    def drain(turn, carry):
        for kind, side in both:
            @pl.when(turn < hops)
            def _():
                add_on(kind, side, turn).wait_send()

            @pl.when(turn >= hops)
            def _():
                pass_on(kind, side, turn).wait_send()
        return carry

    lax.fori_loop(1, 2 * hops, drain, 0)

    def shared(number, carry):
        for side in range(2):
            share(side, number).wait_send()
            share(side, number).wait_recv()
        return carry

    lax.fori_loop(0, count, shared, 0)


def inverse_and_sums(gram, coeff, raw):
    size = gram.shape[0]
    count = coeff.shape[1]
    steps = 2 * (count - 1)
    slots = lambda array: (2, count - 1) + array.shape[2:]
    return pl.pallas_call(
        factor_kernel,
        out_shape=[
            jax.ShapeDtypeStruct((size, size), jnp.bfloat16),
            jax.ShapeDtypeStruct((size, size), jnp.bfloat16),
            jax.ShapeDtypeStruct((2,) + coeff.shape, jnp.bfloat16),
            jax.ShapeDtypeStruct(raw.shape, jnp.bfloat16),
        ],
        in_specs=[pl.BlockSpec(memory_space=pltpu.VMEM)] * 3,
        out_specs=[pl.BlockSpec(memory_space=pltpu.VMEM)] * 4,
        scratch_shapes=[
            pltpu.VMEM((size, size), jnp.float32),
            pltpu.VMEM((BLK, BLK), jnp.float32),
            pltpu.VMEM(slots(coeff), jnp.bfloat16),
            pltpu.VMEM(slots(raw), jnp.bfloat16),
            pltpu.SemaphoreType.DMA((2, 2, steps)),
            pltpu.SemaphoreType.DMA((2, 2, steps)),
            pltpu.SemaphoreType.DMA((2, count)),
            pltpu.SemaphoreType.DMA((2, count)),
        ],
        compiler_params=pltpu.CompilerParams(collective_id=2, has_side_effects=True),
        cost_estimate=pl.CostEstimate(flops=40 * 10 ** 9, bytes_accessed=8 * size * size, transcendentals=0),
    )(gram, coeff, raw)


GROUP = 8


def expert_kernel(high_ref, low_ref, coeff_ref, raw_ref, down_ref, other_ref, back_ref, final, answers, send, recv):
    count, capacity, width = back_ref.shape
    me = lax.axis_index("expert")
    span = GROUP * capacity
    groups = count // GROUP
    barrier = pltpu.get_barrier_semaphore()

    def greet(step, carry):
        pl.semaphore_signal(barrier, inc=1, device_id={"expert": lax.rem(me + step, count)}, device_id_type=MESH)
        return carry

    lax.fori_loop(1, count, greet, 0)
    high = high_ref[...]
    low = low_ref[...]
    for index in range(4):
        block = coeff_ref[index]
        final[index] = (jnp.dot(high, block, preferred_element_type=jnp.float32)
                        + jnp.dot(low, block, preferred_element_type=jnp.float32)).astype(jnp.bfloat16)
    pl.semaphore_wait(barrier, count - 1)

    def give(target):
        return pltpu.make_async_remote_copy(
            src_ref=answers.at[target], dst_ref=back_ref.at[me], send_sem=send.at[target], recv_sem=recv.at[me],
            device_id={"expert": target}, device_id_type=MESH)

    def take(source):
        return pltpu.make_async_remote_copy(
            src_ref=back_ref.at[source], dst_ref=back_ref.at[source], send_sem=send.at[source], recv_sem=recv.at[source],
            device_id={"expert": source}, device_id_type=MESH)

    dims = (((1,), (1,)), ((), ()))

    def compute(turn, carry):
        group = lax.rem(me // GROUP + turn, groups)
        rows = raw_ref[pl.ds(pl.multiple_of(group * span, 16), span), :]
        projected = (lax.dot_general(rows, high_ref[...], dims, preferred_element_type=jnp.float32)
                     + lax.dot_general(rows, low_ref[...], dims, preferred_element_type=jnp.float32)).astype(jnp.bfloat16)
        total = jnp.zeros((span, width), jnp.float32)
        for side, rows_ref in enumerate((down_ref, other_ref)):
            gate = jnp.dot(projected, final[2 * side], preferred_element_type=jnp.float32)
            up = jnp.dot(projected, final[2 * side + 1], preferred_element_type=jnp.float32)
            hidden = (gate / (1.0 + jnp.exp(-gate)) * up).astype(jnp.bfloat16)
            total = total + jnp.dot(hidden, rows_ref[...], preferred_element_type=jnp.float32)
        for index in range(GROUP):
            target = group * GROUP + index
            value = total[index * capacity:(index + 1) * capacity].astype(jnp.bfloat16)

            @pl.when(target == me)
            def _():
                back_ref[me] = value

            @pl.when(target != me)
            def _():
                answers[target] = value
                give(target).start()
        return carry

    lax.fori_loop(0, groups, compute, 0)

    def drain(step, carry):
        take(lax.rem(me + step, count)).wait_recv()
        give(lax.rem(me + step, count)).wait_send()
        return carry

    lax.fori_loop(1, count, drain, 0)


def expert_answers(high, low, coeff, raw, down, other, count, capacity):
    rank = high.shape[0]
    width = down.shape[1]
    return pl.pallas_call(
        expert_kernel,
        out_shape=jax.ShapeDtypeStruct((count, capacity, width), jnp.bfloat16),
        in_specs=[pl.BlockSpec(memory_space=pltpu.VMEM)] * 6,
        out_specs=pl.BlockSpec(memory_space=pltpu.VMEM),
        scratch_shapes=[
            pltpu.VMEM((4, rank, rank), jnp.bfloat16),
            pltpu.VMEM((count, capacity, width), jnp.bfloat16),
            pltpu.SemaphoreType.DMA((count,)),
            pltpu.SemaphoreType.DMA((count,)),
        ],
        compiler_params=pltpu.CompilerParams(collective_id=4, has_side_effects=True),
        cost_estimate=pl.CostEstimate(flops=20 * 10 ** 9, bytes_accessed=8 * rank * rank, transcendentals=0),
    )(high, low, coeff, raw, down, other)


def transposed_dot(left, right):
    return lax.dot_general(left, right, (((0,), (0,)), ((), ())), preferred_element_type=jnp.float32)


def on_device(tokens, gate_weight, up_weight, down_weight, sketch, clusters, routes, route_weights):
    gate_rows = gate_weight[0]
    up_rows = up_weight[0]
    experts = lax.axis_size("expert")
    tensors = lax.axis_size("tensor")
    half = lax.axis_index("dp")
    sketched = jnp.dot(gate_rows, sketch[0, 0], preferred_element_type=jnp.float32) + jnp.dot(
        up_rows, sketch[0, 1], preferred_element_type=jnp.float32
    )
    rank = sketched.shape[1]

    summed = cluster_sum(sketched, clusters)

    tok_rows, width = tokens.shape
    top_count = routes.shape[1]
    capacity = tok_rows * top_count * 3 // (2 * experts)
    named = routes.T[None] == jnp.arange(experts, dtype=jnp.int32)[:, None, None]
    chosen = jnp.any(named, axis=1)
    shares = jnp.sum(jnp.where(named, route_weights.T[None], 0.0), axis=1)
    token_index = jnp.arange(tok_rows)
    earlier = (token_index[:, None] < token_index[None, :]).astype(jnp.bfloat16)
    place = jnp.dot(chosen.astype(jnp.bfloat16), earlier, preferred_element_type=jnp.float32).astype(jnp.int32)
    holds = chosen[:, None, :] & (place[:, None, :] == jnp.arange(capacity, dtype=jnp.int32)[None, :, None])
    select = holds.astype(jnp.bfloat16).reshape(experts * capacity, tok_rows)
    outgoing = jnp.dot(select, tokens, preferred_element_type=jnp.float32).astype(jnp.bfloat16)
    outgoing = outgoing.reshape(experts, capacity, width)

    columns = lax.dynamic_slice_in_dim(summed, half * (rank // 2), rank // 2, 1)
    gram = transposed_dot(summed, columns).reshape(tensors, rank // tensors, rank // 2)
    coeff = jnp.stack([transposed_dot(summed, gate_rows), transposed_dot(summed, up_rows)]).astype(jnp.bfloat16)
    coeff = coeff.reshape(2, tensors, rank // tensors, coeff.shape[2])
    gram, outgoing, coeff = lax.optimization_barrier((gram, outgoing, coeff))
    arrived = lax.all_to_all(outgoing, "expert", split_axis=0, concat_axis=0, tiled=True)
    gram, down_other = gram_sum(gram, down_weight[0])
    arrived, gram = lax.optimization_barrier((arrived, gram))
    raw = jnp.dot(arrived.reshape(experts * capacity, width), summed, preferred_element_type=jnp.float32)
    raw = raw.astype(jnp.bfloat16).reshape(2, tensors, experts * capacity // (2 * tensors), rank)
    high, low, coeff, raw = inverse_and_sums(gram, coeff, raw)
    returned = expert_answers(
        high, low, coeff.reshape(4, rank, -1), raw.reshape(experts * capacity, rank),
        down_weight[0], down_other, experts, capacity)
    returned = returned.reshape(experts * capacity, width)
    mixing = jnp.where(holds, shares[:, None, :], 0.0).reshape(experts * capacity, tok_rows)
    high = mixing.astype(jnp.bfloat16)
    low = (mixing - high.astype(jnp.float32)).astype(jnp.bfloat16)
    return (transposed_dot(high, returned) + transposed_dot(low, returned)).astype(jnp.bfloat16)


def solution(mesh):
    return jax.shard_map(
        on_device,
        mesh=mesh,
        in_specs=(
            P(("expert", "dp"), "tensor"),
            P("expert", "tensor", "dp"),
            P("expert", "tensor", "dp"),
            P("expert", "dp", "tensor"),
            P("expert", None, "dp", None),
            P(),
            P(("expert", "dp"), None),
            P(("expert", "dp"), None),
        ),
        out_specs=P(("expert", "dp"), "tensor"),
        check_vma=False,
    )
```

```python
import jax
import jax.numpy as jnp
from jax import lax
from jax.experimental import pallas as pl
from jax.experimental.pallas import tpu as pltpu
from jax.sharding import PartitionSpec as P

MESH = pl.DeviceIdType.MESH
HIGHEST = lax.Precision.HIGHEST
BLK = 128


def factor_block(tiles, serve):
    lane = lax.broadcasted_iota(jnp.int32, (8, BLK), 1)
    sub = lax.broadcasted_iota(jnp.int32, (8, BLK), 0)
    n = BLK // 8
    tiles = list(tiles)
    for k in range(0, BLK, 2):
        t, r = divmod(k, 8)
        cur = tiles[t]
        col1 = jnp.broadcast_to(cur[:, k:k + 1], (8, BLK))
        col2 = jnp.broadcast_to(cur[:, k + 1:k + 2], (8, BLK))
        a = col1[r:r + 1, :]
        b = col1[r + 1:r + 2, :]
        c = col2[r + 1:r + 2, :]
        ra = 1.0 / a
        rc = a / (a * c - b * b)
        first, second = lane == k, lane == k + 1
        both = jnp.logical_or(first, second)
        row1 = jnp.where(first[:1], 1.0, jnp.where(second[:1], 0.0, cur[r:r + 1, :]))
        row2 = jnp.where(both[:1], 0.0, cur[r + 1:r + 2, :]) - (b * ra) * row1
        row2 = jnp.where(second[:1], 1.0, row2)
        v2 = rc * row2
        v1 = ra * row1 - (b * ra) * v2
        for i in range(t, n):
            old = tiles[i]
            if i == t:
                new = jnp.where(both, 0.0, old) - col1 * v1 - col2 * v2
                new = jnp.where(sub > r + 1, new, old)
                new = jnp.where(sub == r, row1 * jnp.sqrt(ra), new)
                new = jnp.where(sub == r + 1, row2 * jnp.sqrt(rc), new)
            else:
                c1 = jnp.broadcast_to(old[:, k:k + 1], (8, BLK))
                c2 = jnp.broadcast_to(old[:, k + 1:k + 2], (8, BLK))
                new = jnp.where(both, 0.0, old) - c1 * v1 - c2 * v2
            tiles[i] = new
        if k % 32 == 30:
            serve(k // 32)
    return [jnp.where(lane <= sub + 8 * i, tiles[i], 0.0) for i in range(n)]

def eliminate(out_ref, inv_ref, serve):
    size = out_ref.shape[0]
    steps = size // BLK

    def step(j, carry):
        at = pl.multiple_of(j * BLK, BLK)
        tiles = [out_ref[pl.ds(pl.multiple_of(at + 8 * i, 8), 8), pl.ds(at, BLK)] for i in range(BLK // 8)]
        for i, tile in enumerate(factor_block(tiles, lambda turn: serve(turn % 2, 2 * j + turn // 2))):
            inv_ref[8 * i:8 * i + 8, :] = tile
        inv = inv_ref[...]
        rows = lax.broadcasted_iota(jnp.int32, (BLK, BLK), 0)
        cols = lax.broadcasted_iota(jnp.int32, (BLK, BLK), 1)
        eye = jnp.where(rows == cols, 1.0, 0.0)
        out_ref[pl.ds(at, BLK), pl.ds(at, BLK)] = eye
        full = jnp.dot(inv, out_ref[pl.ds(at, BLK), :], precision=HIGHEST, preferred_element_type=jnp.float32)
        column = lax.broadcasted_iota(jnp.int32, (BLK, size), 1)
        later = jnp.where(column >= at + BLK, full, 0.0)
        out_ref[pl.ds(at, BLK), :] = full
        column = lax.broadcasted_iota(jnp.int32, (size, size), 1)
        row = lax.broadcasted_iota(jnp.int32, (size, size), 0)
        zero = (column >= at) & (column < at + BLK) & (row >= at + BLK)
        out_ref[...] = jnp.where(zero, 0.0, out_ref[...]) - lax.dot_general(
            later, full, (((0,), (0,)), ((), ())), precision=HIGHEST, preferred_element_type=jnp.float32)
        return carry

    lax.fori_loop(0, steps, step, 0)
    row = lax.broadcasted_iota(jnp.int32, (size, size), 0)
    column = lax.broadcasted_iota(jnp.int32, (size, size), 1)
    out_ref[...] = jnp.where(column <= row, out_ref[...], 0.0)

REACH = 3
CUTS = 7


def cluster_kernel(part_ref, cluster_ref, out_ref, stage, got, own, plus, minus, acc,
                   dp_send, dp_recv, up_send, up_recv, low_send, low_recv, fin_send, fin_recv):
    count = lax.axis_size("expert")
    me = lax.axis_index("expert")
    half = lax.axis_index("dp")
    sibling = {"dp": 1 - half}
    after = {"expert": lax.rem(me + 1, count)}
    before = {"expert": lax.rem(me + count - 1, count)}
    part = part_ref.shape[0] // 2
    size = part // CUTS
    mine = cluster_ref[me]

    def share(step):
        other = me + step
        inside = jnp.logical_and(other >= 0, other < count)
        same = cluster_ref[lax.rem(other + count, count)] == mine
        return jnp.where(jnp.logical_and(inside, same), 1.0, 0.0).astype(jnp.float32)

    barrier = pltpu.get_barrier_semaphore()
    for device in (sibling, after, before):
        pl.semaphore_signal(barrier, inc=1, device_id=device, device_id_type=MESH)

    def rows(side, cut):
        return pl.ds(pl.multiple_of(side * part + cut * size, 16), size)

    def remote(src, dst, send, recv, device):
        return pltpu.make_async_remote_copy(
            src_ref=src, dst_ref=dst, send_sem=send, recv_sem=recv, device_id=device, device_id_type=MESH)

    def swap(cut):
        return remote(stage.at[cut], got.at[cut], dp_send.at[cut], dp_recv.at[cut], sibling)

    def ahead(hop, cut):
        source = own.at[cut] if hop == 0 else plus.at[hop - 1, cut]
        return remote(source, plus.at[hop, cut], up_send.at[hop, cut], up_recv.at[hop, cut], after)

    def back(hop, cut):
        source = own.at[cut] if hop == 0 else minus.at[hop - 1, cut]
        return remote(source, minus.at[hop, cut], low_send.at[hop, cut], low_recv.at[hop, cut], before)

    def finish(cut):
        place = out_ref.at[rows(half, cut)]
        return remote(place, place, fin_send.at[cut], fin_recv.at[cut], sibling)

    for cut in range(CUTS):
        stage[cut] = part_ref[rows(1 - half, cut), :].astype(jnp.bfloat16)
    pl.semaphore_wait(barrier, 3)
    for cut in range(CUTS):
        swap(cut).start()
    for cut in range(CUTS):
        swap(cut).wait_recv()
        value = (part_ref[rows(half, cut), :] + got[cut].astype(jnp.float32)).astype(jnp.bfloat16)
        own[cut] = value
        ahead(0, cut).start()
        back(0, cut).start()
        acc[cut] = value.astype(jnp.float32)
    for hop in range(REACH):
        for cut in range(CUTS):
            ahead(hop, cut).wait_recv()
            if hop < REACH - 1:
                ahead(hop + 1, cut).start()
            back(hop, cut).wait_recv()
            if hop < REACH - 1:
                back(hop + 1, cut).start()
            total = acc[cut] + share(-1 - hop) * plus[hop, cut].astype(jnp.float32)
            total = total + share(hop + 1) * minus[hop, cut].astype(jnp.float32)
            if hop < REACH - 1:
                acc[cut] = total
            else:
                out_ref[rows(half, cut), :] = total.astype(jnp.bfloat16)
                finish(cut).start()
    for cut in range(CUTS):
        finish(cut).wait_recv()
        finish(cut).wait_send()
        swap(cut).wait_send()
        for hop in range(REACH):
            ahead(hop, cut).wait_send()
            back(hop, cut).wait_send()


def cluster_sum(sketched, clusters):
    rows, rank = sketched.shape
    size = rows // 2 // CUTS
    return pl.pallas_call(
        cluster_kernel,
        out_shape=jax.ShapeDtypeStruct((rows, rank), jnp.bfloat16),
        in_specs=[pl.BlockSpec(memory_space=pltpu.VMEM), pl.BlockSpec(memory_space=pltpu.SMEM)],
        out_specs=pl.BlockSpec(memory_space=pltpu.VMEM),
        scratch_shapes=[
            pltpu.VMEM((CUTS, size, rank), jnp.bfloat16),
            pltpu.VMEM((CUTS, size, rank), jnp.bfloat16),
            pltpu.VMEM((CUTS, size, rank), jnp.bfloat16),
            pltpu.VMEM((REACH, CUTS, size, rank), jnp.bfloat16),
            pltpu.VMEM((REACH, CUTS, size, rank), jnp.bfloat16),
            pltpu.VMEM((CUTS, size, rank), jnp.float32),
            pltpu.SemaphoreType.DMA((CUTS,)),
            pltpu.SemaphoreType.DMA((CUTS,)),
            pltpu.SemaphoreType.DMA((REACH, CUTS)),
            pltpu.SemaphoreType.DMA((REACH, CUTS)),
            pltpu.SemaphoreType.DMA((REACH, CUTS)),
            pltpu.SemaphoreType.DMA((REACH, CUTS)),
            pltpu.SemaphoreType.DMA((CUTS,)),
            pltpu.SemaphoreType.DMA((CUTS,)),
        ],
        compiler_params=pltpu.CompilerParams(collective_id=3, has_side_effects=True),
        cost_estimate=pl.CostEstimate(flops=10 ** 10, bytes_accessed=8 * rows * rank, transcendentals=0),
    )(sketched, clusters)


def gram_kernel(part_ref, down_ref, out_ref, other_ref, arrive, pieces, rs_send, rs_recv, ag_send, ag_recv, sib_send, sib_recv, down_send, down_recv):
    me = lax.axis_index("tensor")
    half = lax.axis_index("dp")
    count = part_ref.shape[0]
    height, width = part_ref.shape[1:]
    sibling = {"dp": 1 - half}
    barrier = pltpu.get_barrier_semaphore()
    for step in range(1, count):
        pl.semaphore_signal(barrier, inc=1, device_id={"tensor": lax.rem(me + step, count)}, device_id_type=MESH)
    pl.semaphore_signal(barrier, inc=1, device_id=sibling, device_id_type=MESH)
    pl.semaphore_wait(barrier, count)

    def scatter(step):
        peer = lax.rem(me + step, count)
        return pltpu.make_async_remote_copy(
            src_ref=part_ref.at[peer], dst_ref=arrive.at[step], send_sem=rs_send.at[step], recv_sem=rs_recv.at[step],
            device_id={"tensor": peer}, device_id_type=MESH)

    def spread(step):
        peer = lax.rem(me + step, count)
        mine = half * count + me
        return pltpu.make_async_remote_copy(
            src_ref=pieces.at[mine], dst_ref=pieces.at[mine], send_sem=ag_send.at[step], recv_sem=ag_recv.at[step],
            device_id={"tensor": peer}, device_id_type=MESH)

    def hand(step):
        piece = half * count + lax.rem(me + count - step, count)
        return pltpu.make_async_remote_copy(
            src_ref=pieces.at[piece], dst_ref=pieces.at[piece], send_sem=sib_send.at[step], recv_sem=sib_recv.at[step],
            device_id=sibling, device_id_type=MESH)

    down = pltpu.make_async_remote_copy(
        src_ref=down_ref, dst_ref=other_ref, send_sem=down_send, recv_sem=down_recv,
        device_id=sibling, device_id_type=MESH)
    order = [4, 3, 5, 2, 6, 1, 7]
    for step in order:
        scatter(step).start()
    down.start()
    total = part_ref[me]
    for step in reversed(order):
        scatter(step).wait_recv()
        total = total + arrive[step]
    pieces[half * count + me] = total
    for step in order:
        spread(step).start()
    hand(0).start()
    for step in reversed(order):
        spread(step).wait_recv()
        hand(step).start()
    for step in range(count):
        hand(step).wait_recv()
    for side in range(2):
        for piece in range(count):
            out_ref[piece * height:(piece + 1) * height, side * width:(side + 1) * width] = pieces[side * count + piece]
    for step in order:
        scatter(step).wait_send()
        spread(step).wait_send()
    for step in range(count):
        hand(step).wait_send()
    down.wait()


def gram_sum(part, down):
    count, height, width = part.shape
    size = count * height
    return pl.pallas_call(
        gram_kernel,
        out_shape=[jax.ShapeDtypeStruct((size, size), jnp.float32), jax.ShapeDtypeStruct(down.shape, down.dtype)],
        in_specs=[pl.BlockSpec(memory_space=pltpu.VMEM), pl.BlockSpec(memory_space=pl.ANY)],
        out_specs=[pl.BlockSpec(memory_space=pltpu.VMEM), pl.BlockSpec(memory_space=pl.ANY)],
        scratch_shapes=[
            pltpu.VMEM((count, height, width), jnp.float32),
            pltpu.VMEM((2 * count, height, width), jnp.float32),
        ] + [pltpu.SemaphoreType.DMA((count,))] * 6 + [pltpu.SemaphoreType.DMA] * 2,
        compiler_params=pltpu.CompilerParams(collective_id=1, has_side_effects=True),
        cost_estimate=pl.CostEstimate(flops=40 * 10 ** 9, bytes_accessed=8 * size * size, transcendentals=0),
    )(part, down)


def factor_kernel(gram_ref, coeff_ref, raw_ref, high_ref, low_ref, coeff_all, raw_all, out_ref, inv_ref, coeff_slot, raw_slot,
                  send, recv, sib_send, sib_recv):
    count = coeff_ref.shape[0]
    longer = count // 2
    reach = (longer, longer - 1)
    me = lax.axis_index("tensor")
    half = lax.axis_index("dp")
    sibling = {"dp": 1 - half}
    after = {"tensor": lax.rem(me + 1, count)}
    before = {"tensor": lax.rem(me + count - 1, count)}
    parts, slots = (coeff_ref, raw_ref), (coeff_slot, raw_slot)
    barrier = pltpu.get_barrier_semaphore()
    for device in (sibling, after, before):
        pl.semaphore_signal(barrier, inc=1, device_id=device, device_id_type=MESH)
    pl.semaphore_wait(barrier, 3)

    def upward(kind, side):
        return kind == side

    def chunk(kind, side, distance):
        return lax.rem(me + (distance if upward(kind, side) else count - distance), count)

    def place(kind, index):
        return coeff_all.at[0, index] if kind == 0 else raw_all.at[index]

    def remote(src, dst, kind, side, turn):
        return pltpu.make_async_remote_copy(
            src_ref=src, dst_ref=dst, send_sem=send.at[kind, side, turn], recv_sem=recv.at[kind, side, turn],
            device_id=after if upward(kind, side) else before, device_id_type=MESH)

    def first(kind, side):
        return remote(parts[kind].at[chunk(kind, side, reach[side])], slots[kind].at[side, 0], kind, side, 0)

    def add_on(kind, side, turn):
        return remote(slots[kind].at[side, turn - 1], slots[kind].at[side, turn], kind, side, turn)

    def pass_on(kind, side, hop):
        here = place(kind, lax.rem(me + (count - hop if upward(kind, side) else hop), count))
        return remote(here, here, kind, side, longer + hop)

    def share(index):
        return pltpu.make_async_remote_copy(
            src_ref=coeff_all.at[0, index], dst_ref=coeff_all.at[1, index], send_sem=sib_send.at[index],
            recv_sem=sib_recv.at[index], device_id=sibling, device_id_type=MESH)

    for kind in range(2):
        for side in range(2):
            first(kind, side).start()

    def serve(kind, turn):
        for side in range(2):
            @pl.when(turn < reach[side])
            def _():
                slot = slots[kind].at[side, turn]
                remote(slot, slot, kind, side, turn).wait_recv()

            @pl.when(turn < reach[side] - 1)
            def _():
                part = parts[kind][chunk(kind, side, reach[side] - 1 - turn)]
                value = slots[kind][side, turn].astype(jnp.float32) + part.astype(jnp.float32)
                slots[kind][side, turn] = value.astype(jnp.bfloat16)
                add_on(kind, side, turn + 1).start()

        @pl.when(turn == longer - 1)
        def _():
            value = parts[kind][me].astype(jnp.float32) + slots[kind][0, longer - 1].astype(jnp.float32)
            value = value + slots[kind][1, longer - 2].astype(jnp.float32)
            place(kind, me)[...] = value.astype(jnp.bfloat16)
            for side in range(2):
                pass_on(kind, side, 0).start()
            if kind == 0:
                share(me).start()

        hop = turn - longer
        for side in range(2):
            index = lax.rem(me + (2 * count - 1 - hop if upward(kind, side) else hop + 1), count)

            @pl.when((hop >= 0) & (hop < reach[side]))
            def _():
                remote(place(kind, index), place(kind, index), kind, side, turn).wait_recv()
                if kind == 0:
                    share(index).start()

            @pl.when((hop >= 0) & (hop < reach[side] - 1))
            def _():
                pass_on(kind, side, hop + 1).start()

    out_ref[...] = gram_ref[...]
    eliminate(out_ref, inv_ref, serve)
    high = out_ref[...].astype(jnp.bfloat16)
    high_ref[...] = high
    low_ref[...] = (out_ref[...] - high.astype(jnp.float32)).astype(jnp.bfloat16)

    for kind in range(2):
        for side in range(2):
            first(kind, side).wait_send()
            for turn in range(1, reach[side]):
                add_on(kind, side, turn).wait_send()
            for hop in range(reach[side]):
                pass_on(kind, side, hop).wait_send()

    def shared(index, carry):
        share(index).wait_send()
        share(index).wait_recv()
        return carry

    lax.fori_loop(0, count, shared, 0)


def inverse_and_sums(gram, coeff, raw):
    size = gram.shape[0]
    count = coeff.shape[0]
    slots = lambda array: (2, count // 2) + array.shape[1:]
    return pl.pallas_call(
        factor_kernel,
        out_shape=[
            jax.ShapeDtypeStruct((size, size), jnp.bfloat16),
            jax.ShapeDtypeStruct((size, size), jnp.bfloat16),
            jax.ShapeDtypeStruct((2,) + coeff.shape, jnp.bfloat16),
            jax.ShapeDtypeStruct(raw.shape, jnp.bfloat16),
        ],
        in_specs=[pl.BlockSpec(memory_space=pltpu.VMEM)] * 3,
        out_specs=[pl.BlockSpec(memory_space=pltpu.VMEM)] * 4,
        scratch_shapes=[
            pltpu.VMEM((size, size), jnp.float32),
            pltpu.VMEM((BLK, BLK), jnp.float32),
            pltpu.VMEM(slots(coeff), jnp.bfloat16),
            pltpu.VMEM(slots(raw), jnp.bfloat16),
            pltpu.SemaphoreType.DMA((2, 2, count)),
            pltpu.SemaphoreType.DMA((2, 2, count)),
            pltpu.SemaphoreType.DMA((count,)),
            pltpu.SemaphoreType.DMA((count,)),
        ],
        compiler_params=pltpu.CompilerParams(collective_id=2, has_side_effects=True),
        cost_estimate=pl.CostEstimate(flops=40 * 10 ** 9, bytes_accessed=8 * size * size, transcendentals=0),
    )(gram, coeff, raw)


GROUP = 8


def expert_kernel(high_ref, low_ref, coeff_ref, raw_ref, down_ref, other_ref, back_ref, final, answers, send, recv):
    count, capacity, width = back_ref.shape
    me = lax.axis_index("expert")
    span = GROUP * capacity
    groups = count // GROUP
    barrier = pltpu.get_barrier_semaphore()

    def greet(step, carry):
        pl.semaphore_signal(barrier, inc=1, device_id={"expert": lax.rem(me + step, count)}, device_id_type=MESH)
        return carry

    lax.fori_loop(1, count, greet, 0)
    high = high_ref[...]
    low = low_ref[...]
    for index in range(4):
        side, pick = divmod(index, 2)
        block = jnp.concatenate([coeff_ref[side, piece, pick] for piece in range(coeff_ref.shape[1])], axis=0)
        final[index] = (jnp.dot(high, block, preferred_element_type=jnp.float32)
                        + jnp.dot(low, block, preferred_element_type=jnp.float32)).astype(jnp.bfloat16)
    pl.semaphore_wait(barrier, count - 1)

    def give(target):
        return pltpu.make_async_remote_copy(
            src_ref=answers.at[target], dst_ref=back_ref.at[me], send_sem=send.at[target], recv_sem=recv.at[me],
            device_id={"expert": target}, device_id_type=MESH)

    def take(source):
        return pltpu.make_async_remote_copy(
            src_ref=back_ref.at[source], dst_ref=back_ref.at[source], send_sem=send.at[source], recv_sem=recv.at[source],
            device_id={"expert": source}, device_id_type=MESH)

    dims = (((1,), (1,)), ((), ()))

    def compute(turn, carry):
        group = lax.rem(me // GROUP + turn, groups)
        rows = raw_ref[pl.ds(pl.multiple_of(group * span, 16), span), :]
        projected = (lax.dot_general(rows, high_ref[...], dims, preferred_element_type=jnp.float32)
                     + lax.dot_general(rows, low_ref[...], dims, preferred_element_type=jnp.float32)).astype(jnp.bfloat16)
        total = jnp.zeros((span, width), jnp.float32)
        for side, rows_ref in enumerate((down_ref, other_ref)):
            gate = jnp.dot(projected, final[2 * side], preferred_element_type=jnp.float32)
            up = jnp.dot(projected, final[2 * side + 1], preferred_element_type=jnp.float32)
            hidden = (gate / (1.0 + jnp.exp(-gate)) * up).astype(jnp.bfloat16)
            total = total + jnp.dot(hidden, rows_ref[...], preferred_element_type=jnp.float32)
        for index in range(GROUP):
            target = group * GROUP + index
            value = total[index * capacity:(index + 1) * capacity].astype(jnp.bfloat16)

            @pl.when(target == me)
            def _():
                back_ref[me] = value

            @pl.when(target != me)
            def _():
                answers[target] = value
                give(target).start()
        return carry

    lax.fori_loop(0, groups, compute, 0)

    def drain(step, carry):
        take(lax.rem(me + step, count)).wait_recv()
        give(lax.rem(me + step, count)).wait_send()
        return carry

    lax.fori_loop(1, count, drain, 0)


def expert_answers(high, low, coeff, raw, down, other, count, capacity):
    rank = high.shape[0]
    width = down.shape[1]
    return pl.pallas_call(
        expert_kernel,
        out_shape=jax.ShapeDtypeStruct((count, capacity, width), jnp.bfloat16),
        in_specs=[pl.BlockSpec(memory_space=pltpu.VMEM)] * 6,
        out_specs=pl.BlockSpec(memory_space=pltpu.VMEM),
        scratch_shapes=[
            pltpu.VMEM((4, rank, rank), jnp.bfloat16),
            pltpu.VMEM((count, capacity, width), jnp.bfloat16),
            pltpu.SemaphoreType.DMA((count,)),
            pltpu.SemaphoreType.DMA((count,)),
        ],
        compiler_params=pltpu.CompilerParams(collective_id=4, has_side_effects=True),
        cost_estimate=pl.CostEstimate(flops=20 * 10 ** 9, bytes_accessed=8 * rank * rank, transcendentals=0),
    )(high, low, coeff, raw, down, other)


def transposed_dot(left, right):
    return lax.dot_general(left, right, (((0,), (0,)), ((), ())), preferred_element_type=jnp.float32)


def on_device(tokens, gate_weight, up_weight, down_weight, sketch, clusters, routes, route_weights):
    gate_rows = gate_weight[0]
    up_rows = up_weight[0]
    experts = lax.axis_size("expert")
    tensors = lax.axis_size("tensor")
    half = lax.axis_index("dp")
    sketched = jnp.dot(gate_rows, sketch[0, 0], preferred_element_type=jnp.float32) + jnp.dot(
        up_rows, sketch[0, 1], preferred_element_type=jnp.float32
    )
    rank = sketched.shape[1]

    summed = cluster_sum(sketched, clusters)

    tok_rows, width = tokens.shape
    top_count = routes.shape[1]
    capacity = tok_rows * top_count * 3 // (2 * experts)
    named = routes.T[None] == jnp.arange(experts, dtype=jnp.int32)[:, None, None]
    chosen = jnp.any(named, axis=1)
    shares = jnp.sum(jnp.where(named, route_weights.T[None], 0.0), axis=1)
    token_index = jnp.arange(tok_rows)
    earlier = (token_index[:, None] < token_index[None, :]).astype(jnp.bfloat16)
    place = jnp.dot(chosen.astype(jnp.bfloat16), earlier, preferred_element_type=jnp.float32).astype(jnp.int32)
    holds = chosen[:, None, :] & (place[:, None, :] == jnp.arange(capacity, dtype=jnp.int32)[None, :, None])
    select = holds.astype(jnp.bfloat16).reshape(experts * capacity, tok_rows)
    outgoing = jnp.dot(select, tokens, preferred_element_type=jnp.float32).astype(jnp.bfloat16)
    outgoing = outgoing.reshape(experts, capacity, width)

    columns = lax.dynamic_slice_in_dim(summed, half * (rank // 2), rank // 2, 1)
    gram = transposed_dot(summed, columns).reshape(tensors, rank // tensors, rank // 2)
    coeff = [transposed_dot(summed, rows).reshape(tensors, rank // tensors, -1) for rows in (gate_rows, up_rows)]
    coeff = jnp.stack(coeff, axis=1).astype(jnp.bfloat16)
    gram, outgoing, coeff = lax.optimization_barrier((gram, outgoing, coeff))
    arrived = lax.all_to_all(outgoing, "expert", split_axis=0, concat_axis=0, tiled=True)
    gram, down_other = gram_sum(gram, down_weight[0])
    arrived, gram = lax.optimization_barrier((arrived, gram))
    raw = jnp.dot(arrived.reshape(experts * capacity, width), summed, preferred_element_type=jnp.float32)
    raw = raw.astype(jnp.bfloat16).reshape(tensors, experts * capacity // tensors, rank)
    high, low, coeff, raw = inverse_and_sums(gram, coeff, raw)
    returned = expert_answers(
        high, low, coeff, raw.reshape(experts * capacity, rank),
        down_weight[0], down_other, experts, capacity)
    returned = returned.reshape(experts * capacity, width)
    mixing = jnp.where(holds, shares[:, None, :], 0.0).reshape(experts * capacity, tok_rows)
    high = mixing.astype(jnp.bfloat16)
    low = (mixing - high.astype(jnp.float32)).astype(jnp.bfloat16)
    return (transposed_dot(high, returned) + transposed_dot(low, returned)).astype(jnp.bfloat16)


def solution(mesh):
    return jax.shard_map(
        on_device,
        mesh=mesh,
        in_specs=(
            P(("expert", "dp"), "tensor"),
            P("expert", "tensor", "dp"),
            P("expert", "tensor", "dp"),
            P("expert", "dp", "tensor"),
            P("expert", None, "dp", None),
            P(),
            P(("expert", "dp"), None),
            P(("expert", "dp"), None),
        ),
        out_specs=P(("expert", "dp"), "tensor"),
        check_vma=False,
    )
```

```python
import jax
import jax.numpy as jnp
from jax import lax
from jax.experimental import pallas as pl
from jax.experimental.pallas import tpu as pltpu
from jax.sharding import PartitionSpec as P

MESH = pl.DeviceIdType.MESH
HIGHEST = lax.Precision.HIGHEST
BLK = 128


def factor_block(tiles, serve):
    lane = lax.broadcasted_iota(jnp.int32, (8, BLK), 1)
    sub = lax.broadcasted_iota(jnp.int32, (8, BLK), 0)
    n = BLK // 8
    tiles = list(tiles)
    for k in range(0, BLK, 2):
        t, r = divmod(k, 8)
        cur = tiles[t]
        col1 = jnp.broadcast_to(cur[:, k:k + 1], (8, BLK))
        col2 = jnp.broadcast_to(cur[:, k + 1:k + 2], (8, BLK))
        a = col1[r:r + 1, :]
        b = col1[r + 1:r + 2, :]
        c = col2[r + 1:r + 2, :]
        ra = 1.0 / a
        rc = a / (a * c - b * b)
        first, second = lane == k, lane == k + 1
        both = jnp.logical_or(first, second)
        row1 = jnp.where(first[:1], 1.0, jnp.where(second[:1], 0.0, cur[r:r + 1, :]))
        row2 = jnp.where(both[:1], 0.0, cur[r + 1:r + 2, :]) - (b * ra) * row1
        row2 = jnp.where(second[:1], 1.0, row2)
        v2 = rc * row2
        v1 = ra * row1 - (b * ra) * v2
        for i in range(t, n):
            old = tiles[i]
            if i == t:
                new = jnp.where(both, 0.0, old) - col1 * v1 - col2 * v2
                new = jnp.where(sub > r + 1, new, old)
                new = jnp.where(sub == r, row1 * jnp.sqrt(ra), new)
                new = jnp.where(sub == r + 1, row2 * jnp.sqrt(rc), new)
            else:
                c1 = jnp.broadcast_to(old[:, k:k + 1], (8, BLK))
                c2 = jnp.broadcast_to(old[:, k + 1:k + 2], (8, BLK))
                new = jnp.where(both, 0.0, old) - c1 * v1 - c2 * v2
            tiles[i] = new
        if k % 32 == 30:
            serve(k // 32)
    return [jnp.where(lane <= sub + 8 * i, tiles[i], 0.0) for i in range(n)]

def eliminate(out_ref, inv_ref, serve):
    size = out_ref.shape[0]
    steps = size // BLK

    def step(j, carry):
        at = pl.multiple_of(j * BLK, BLK)
        tiles = [out_ref[pl.ds(pl.multiple_of(at + 8 * i, 8), 8), pl.ds(at, BLK)] for i in range(BLK // 8)]
        for i, tile in enumerate(factor_block(tiles, lambda turn: serve(turn % 2, 2 * j + turn // 2))):
            inv_ref[8 * i:8 * i + 8, :] = tile
        inv = inv_ref[...]
        rows = lax.broadcasted_iota(jnp.int32, (BLK, BLK), 0)
        cols = lax.broadcasted_iota(jnp.int32, (BLK, BLK), 1)
        eye = jnp.where(rows == cols, 1.0, 0.0)
        out_ref[pl.ds(at, BLK), pl.ds(at, BLK)] = eye
        full = jnp.dot(inv, out_ref[pl.ds(at, BLK), :], precision=HIGHEST, preferred_element_type=jnp.float32)
        column = lax.broadcasted_iota(jnp.int32, (BLK, size), 1)
        later = jnp.where(column >= at + BLK, full, 0.0)
        out_ref[pl.ds(at, BLK), :] = full
        column = lax.broadcasted_iota(jnp.int32, (size, size), 1)
        row = lax.broadcasted_iota(jnp.int32, (size, size), 0)
        zero = (column >= at) & (column < at + BLK) & (row >= at + BLK)
        out_ref[...] = jnp.where(zero, 0.0, out_ref[...]) - lax.dot_general(
            later, full, (((0,), (0,)), ((), ())), precision=HIGHEST, preferred_element_type=jnp.float32)
        return carry

    lax.fori_loop(0, steps, step, 0)
    row = lax.broadcasted_iota(jnp.int32, (size, size), 0)
    column = lax.broadcasted_iota(jnp.int32, (size, size), 1)
    out_ref[...] = jnp.where(column <= row, out_ref[...], 0.0)

REACH = 3
CUTS = 7


def cluster_kernel(part_ref, cluster_ref, out_ref, stage, got, own, plus, minus, acc,
                   dp_send, dp_recv, up_send, up_recv, low_send, low_recv, fin_send, fin_recv):
    count = lax.axis_size("expert")
    me = lax.axis_index("expert")
    half = lax.axis_index("dp")
    sibling = {"dp": 1 - half}
    after = {"expert": lax.rem(me + 1, count)}
    before = {"expert": lax.rem(me + count - 1, count)}
    part = part_ref.shape[0] // 2
    size = part // CUTS
    mine = cluster_ref[me]

    def share(step):
        other = me + step
        inside = jnp.logical_and(other >= 0, other < count)
        same = cluster_ref[lax.rem(other + count, count)] == mine
        return jnp.where(jnp.logical_and(inside, same), 1.0, 0.0).astype(jnp.float32)

    barrier = pltpu.get_barrier_semaphore()
    for device in (sibling, after, before):
        pl.semaphore_signal(barrier, inc=1, device_id=device, device_id_type=MESH)

    def rows(side, cut):
        return pl.ds(pl.multiple_of(side * part + cut * size, 16), size)

    def remote(src, dst, send, recv, device):
        return pltpu.make_async_remote_copy(
            src_ref=src, dst_ref=dst, send_sem=send, recv_sem=recv, device_id=device, device_id_type=MESH)

    def swap(cut):
        return remote(stage.at[cut], got.at[cut], dp_send.at[cut], dp_recv.at[cut], sibling)

    def ahead(hop, cut):
        source = own.at[cut] if hop == 0 else plus.at[hop - 1, cut]
        return remote(source, plus.at[hop, cut], up_send.at[hop, cut], up_recv.at[hop, cut], after)

    def back(hop, cut):
        source = own.at[cut] if hop == 0 else minus.at[hop - 1, cut]
        return remote(source, minus.at[hop, cut], low_send.at[hop, cut], low_recv.at[hop, cut], before)

    def finish(cut):
        place = out_ref.at[rows(half, cut)]
        return remote(place, place, fin_send.at[cut], fin_recv.at[cut], sibling)

    for cut in range(CUTS):
        stage[cut] = part_ref[rows(1 - half, cut), :].astype(jnp.bfloat16)
    pl.semaphore_wait(barrier, 3)
    for cut in range(CUTS):
        swap(cut).start()
    for cut in range(CUTS):
        swap(cut).wait_recv()
        value = (part_ref[rows(half, cut), :] + got[cut].astype(jnp.float32)).astype(jnp.bfloat16)
        own[cut] = value
        ahead(0, cut).start()
        back(0, cut).start()
        acc[cut] = value.astype(jnp.float32)
    for hop in range(REACH):
        for cut in range(CUTS):
            ahead(hop, cut).wait_recv()
            if hop < REACH - 1:
                ahead(hop + 1, cut).start()
            back(hop, cut).wait_recv()
            if hop < REACH - 1:
                back(hop + 1, cut).start()
            total = acc[cut] + share(-1 - hop) * plus[hop, cut].astype(jnp.float32)
            total = total + share(hop + 1) * minus[hop, cut].astype(jnp.float32)
            if hop < REACH - 1:
                acc[cut] = total
            else:
                out_ref[rows(half, cut), :] = total.astype(jnp.bfloat16)
                finish(cut).start()
    for cut in range(CUTS):
        finish(cut).wait_recv()
        finish(cut).wait_send()
        swap(cut).wait_send()
        for hop in range(REACH):
            ahead(hop, cut).wait_send()
            back(hop, cut).wait_send()


def cluster_sum(sketched, clusters):
    rows, rank = sketched.shape
    size = rows // 2 // CUTS
    return pl.pallas_call(
        cluster_kernel,
        out_shape=jax.ShapeDtypeStruct((rows, rank), jnp.bfloat16),
        in_specs=[pl.BlockSpec(memory_space=pltpu.VMEM), pl.BlockSpec(memory_space=pltpu.SMEM)],
        out_specs=pl.BlockSpec(memory_space=pltpu.VMEM),
        scratch_shapes=[
            pltpu.VMEM((CUTS, size, rank), jnp.bfloat16),
            pltpu.VMEM((CUTS, size, rank), jnp.bfloat16),
            pltpu.VMEM((CUTS, size, rank), jnp.bfloat16),
            pltpu.VMEM((REACH, CUTS, size, rank), jnp.bfloat16),
            pltpu.VMEM((REACH, CUTS, size, rank), jnp.bfloat16),
            pltpu.VMEM((CUTS, size, rank), jnp.float32),
            pltpu.SemaphoreType.DMA((CUTS,)),
            pltpu.SemaphoreType.DMA((CUTS,)),
            pltpu.SemaphoreType.DMA((REACH, CUTS)),
            pltpu.SemaphoreType.DMA((REACH, CUTS)),
            pltpu.SemaphoreType.DMA((REACH, CUTS)),
            pltpu.SemaphoreType.DMA((REACH, CUTS)),
            pltpu.SemaphoreType.DMA((CUTS,)),
            pltpu.SemaphoreType.DMA((CUTS,)),
        ],
        compiler_params=pltpu.CompilerParams(collective_id=3, has_side_effects=True),
        cost_estimate=pl.CostEstimate(flops=10 ** 10, bytes_accessed=8 * rows * rank, transcendentals=0),
    )(sketched, clusters)


def gram_kernel(part_ref, down_ref, send_ref, sum_ref, gate_ref, up_ref, out_ref, other_ref, coeff_ref, raw_ref,
                arrive, pieces, landed, rs_send, rs_recv, ag_send, ag_recv, sib_send, sib_recv, down_send, down_recv,
                tok_send, tok_recv):
    me = lax.axis_index("tensor")
    half = lax.axis_index("dp")
    expert = lax.axis_index("expert")
    experts = send_ref.shape[0]
    count = part_ref.shape[0]
    height, width = part_ref.shape[1:]
    sibling = {"dp": 1 - half}
    barrier = pltpu.get_barrier_semaphore()
    for step in range(1, count):
        pl.semaphore_signal(barrier, inc=1, device_id={"tensor": lax.rem(me + step, count)}, device_id_type=MESH)
    pl.semaphore_signal(barrier, inc=1, device_id=sibling, device_id_type=MESH)

    def greet(step, carry):
        pl.semaphore_signal(barrier, inc=1, device_id={"expert": lax.rem(expert + step, experts)}, device_id_type=MESH)
        return carry

    lax.fori_loop(1, experts, greet, 0)
    pl.semaphore_wait(barrier, count + experts - 1)

    def scatter(step):
        peer = lax.rem(me + step, count)
        return pltpu.make_async_remote_copy(
            src_ref=part_ref.at[peer], dst_ref=arrive.at[step], send_sem=rs_send.at[step], recv_sem=rs_recv.at[step],
            device_id={"tensor": peer}, device_id_type=MESH)

    def spread(step):
        peer = lax.rem(me + step, count)
        mine = half * count + me
        return pltpu.make_async_remote_copy(
            src_ref=pieces.at[mine], dst_ref=pieces.at[mine], send_sem=ag_send.at[step], recv_sem=ag_recv.at[step],
            device_id={"tensor": peer}, device_id_type=MESH)

    def hand(step):
        piece = half * count + lax.rem(me + count - step, count)
        return pltpu.make_async_remote_copy(
            src_ref=pieces.at[piece], dst_ref=pieces.at[piece], send_sem=sib_send.at[step], recv_sem=sib_recv.at[step],
            device_id=sibling, device_id_type=MESH)

    def route(step):
        peer = lax.rem(expert + step, experts)
        return pltpu.make_async_remote_copy(
            src_ref=send_ref.at[peer], dst_ref=landed.at[expert], send_sem=tok_send.at[peer], recv_sem=tok_recv.at[expert],
            device_id={"expert": peer}, device_id_type=MESH)

    def landing(source):
        return pltpu.make_async_remote_copy(
            src_ref=send_ref.at[source], dst_ref=landed.at[source], send_sem=tok_send.at[source],
            recv_sem=tok_recv.at[source], device_id={"expert": source}, device_id_type=MESH)

    down = pltpu.make_async_remote_copy(
        src_ref=down_ref, dst_ref=other_ref, send_sem=down_send, recv_sem=down_recv,
        device_id=sibling, device_id_type=MESH)
    order = [4, 3, 5, 2, 6, 1, 7]
    for step in order:
        scatter(step).start()

    def route_all(step, carry):
        route(step).start()
        return carry

    lax.fori_loop(1, experts, route_all, 0)
    down.start()
    landed[expert] = send_ref[expert]
    turned = (((0,), (0,)), ((), ()))
    block = lax.dot_general(sum_ref[...], gate_ref[...], turned, preferred_element_type=jnp.float32)
    for piece in range(count):
        coeff_ref[piece, 0] = block[piece * height:(piece + 1) * height].astype(jnp.bfloat16)
    block = lax.dot_general(sum_ref[...], up_ref[...], turned, preferred_element_type=jnp.float32)
    for piece in range(count):
        coeff_ref[piece, 1] = block[piece * height:(piece + 1) * height].astype(jnp.bfloat16)
    total = part_ref[me]
    for step in reversed(order):
        scatter(step).wait_recv()
        total = total + arrive[step]
    pieces[half * count + me] = total
    for step in order:
        spread(step).start()
    hand(0).start()
    for step in reversed(order):
        spread(step).wait_recv()
        hand(step).start()
    for step in range(count):
        hand(step).wait_recv()
    for side in range(2):
        for piece in range(count):
            out_ref[piece * height:(piece + 1) * height, side * width:(side + 1) * width] = pieces[side * count + piece]
    for step in order:
        scatter(step).wait_send()
        spread(step).wait_send()
    for step in range(count):
        hand(step).wait_send()
    down.wait()

    def settle(step, carry):
        landing(lax.rem(expert + step, experts)).wait_recv()
        route(step).wait_send()
        return carry

    lax.fori_loop(1, experts, settle, 0)
    capacity = send_ref.shape[1]
    group = raw_ref.shape[1] // capacity

    def project(index, carry):
        rows = jnp.concatenate([landed[index * group + item].astype(jnp.float32) for item in range(group)], axis=0)
        raw_ref[index] = jnp.dot(
            rows.astype(jnp.bfloat16), sum_ref[...], preferred_element_type=jnp.float32).astype(jnp.bfloat16)
        return carry

    lax.fori_loop(0, experts // group, project, 0)


def gram_sum(part, down, outgoing, summed, gate, up):
    count, height, width = part.shape
    size = count * height
    experts, capacity, depth = outgoing.shape
    vmem, any_space = pl.BlockSpec(memory_space=pltpu.VMEM), pl.BlockSpec(memory_space=pl.ANY)
    return pl.pallas_call(
        gram_kernel,
        out_shape=[
            jax.ShapeDtypeStruct((size, size), jnp.float32),
            jax.ShapeDtypeStruct(down.shape, down.dtype),
            jax.ShapeDtypeStruct((count, 2, height, gate.shape[1]), jnp.bfloat16),
            jax.ShapeDtypeStruct((count, experts * capacity // count, size), jnp.bfloat16),
        ],
        in_specs=[vmem, any_space, vmem, vmem, vmem, vmem],
        out_specs=[vmem, any_space, vmem, vmem],
        scratch_shapes=[
            pltpu.VMEM((count, height, width), jnp.float32),
            pltpu.VMEM((2 * count, height, width), jnp.float32),
            pltpu.VMEM((experts, capacity, depth), jnp.bfloat16),
        ] + [pltpu.SemaphoreType.DMA((count,))] * 6 + [pltpu.SemaphoreType.DMA] * 2
        + [pltpu.SemaphoreType.DMA((experts,))] * 2,
        compiler_params=pltpu.CompilerParams(collective_id=1, has_side_effects=True),
        cost_estimate=pl.CostEstimate(flops=40 * 10 ** 9, bytes_accessed=8 * size * size, transcendentals=0),
    )(part, down, outgoing, summed, gate, up)


def factor_kernel(gram_ref, coeff_ref, raw_ref, high_ref, low_ref, coeff_all, raw_all, out_ref, inv_ref, coeff_slot, raw_slot,
                  send, recv, sib_send, sib_recv):
    count = coeff_ref.shape[0]
    longer = count // 2
    reach = (longer, longer - 1)
    me = lax.axis_index("tensor")
    half = lax.axis_index("dp")
    sibling = {"dp": 1 - half}
    after = {"tensor": lax.rem(me + 1, count)}
    before = {"tensor": lax.rem(me + count - 1, count)}
    parts, slots = (coeff_ref, raw_ref), (coeff_slot, raw_slot)
    barrier = pltpu.get_barrier_semaphore()
    for device in (sibling, after, before):
        pl.semaphore_signal(barrier, inc=1, device_id=device, device_id_type=MESH)
    pl.semaphore_wait(barrier, 3)

    def upward(kind, side):
        return kind == side

    def chunk(kind, side, distance):
        return lax.rem(me + (distance if upward(kind, side) else count - distance), count)

    def place(kind, index):
        return coeff_all.at[0, index] if kind == 0 else raw_all.at[index]

    def remote(src, dst, kind, side, turn):
        return pltpu.make_async_remote_copy(
            src_ref=src, dst_ref=dst, send_sem=send.at[kind, side, turn], recv_sem=recv.at[kind, side, turn],
            device_id=after if upward(kind, side) else before, device_id_type=MESH)

    def first(kind, side):
        return remote(parts[kind].at[chunk(kind, side, reach[side])], slots[kind].at[side, 0], kind, side, 0)

    def add_on(kind, side, turn):
        return remote(slots[kind].at[side, turn - 1], slots[kind].at[side, turn], kind, side, turn)

    def pass_on(kind, side, hop):
        here = place(kind, lax.rem(me + (count - hop if upward(kind, side) else hop), count))
        return remote(here, here, kind, side, longer + hop)

    def share(index):
        return pltpu.make_async_remote_copy(
            src_ref=coeff_all.at[0, index], dst_ref=coeff_all.at[1, index], send_sem=sib_send.at[index],
            recv_sem=sib_recv.at[index], device_id=sibling, device_id_type=MESH)

    for kind in range(2):
        for side in range(2):
            first(kind, side).start()

    def serve(kind, turn):
        for side in range(2):
            @pl.when(turn < reach[side])
            def _():
                slot = slots[kind].at[side, turn]
                remote(slot, slot, kind, side, turn).wait_recv()

            @pl.when(turn < reach[side] - 1)
            def _():
                part = parts[kind][chunk(kind, side, reach[side] - 1 - turn)]
                value = slots[kind][side, turn].astype(jnp.float32) + part.astype(jnp.float32)
                slots[kind][side, turn] = value.astype(jnp.bfloat16)
                add_on(kind, side, turn + 1).start()

        @pl.when(turn == longer - 1)
        def _():
            value = parts[kind][me].astype(jnp.float32) + slots[kind][0, longer - 1].astype(jnp.float32)
            value = value + slots[kind][1, longer - 2].astype(jnp.float32)
            place(kind, me)[...] = value.astype(jnp.bfloat16)
            for side in range(2):
                pass_on(kind, side, 0).start()
            if kind == 0:
                share(me).start()

        hop = turn - longer
        for side in range(2):
            index = lax.rem(me + (2 * count - 1 - hop if upward(kind, side) else hop + 1), count)

            @pl.when((hop >= 0) & (hop < reach[side]))
            def _():
                remote(place(kind, index), place(kind, index), kind, side, turn).wait_recv()
                if kind == 0:
                    share(index).start()

            @pl.when((hop >= 0) & (hop < reach[side] - 1))
            def _():
                pass_on(kind, side, hop + 1).start()

    out_ref[...] = gram_ref[...]
    eliminate(out_ref, inv_ref, serve)
    high = out_ref[...].astype(jnp.bfloat16)
    high_ref[...] = high
    low_ref[...] = (out_ref[...] - high.astype(jnp.float32)).astype(jnp.bfloat16)

    for kind in range(2):
        for side in range(2):
            first(kind, side).wait_send()
            for turn in range(1, reach[side]):
                add_on(kind, side, turn).wait_send()
            for hop in range(reach[side]):
                pass_on(kind, side, hop).wait_send()

    def shared(index, carry):
        share(index).wait_send()
        share(index).wait_recv()
        return carry

    lax.fori_loop(0, count, shared, 0)


def inverse_and_sums(gram, coeff, raw):
    size = gram.shape[0]
    count = coeff.shape[0]
    slots = lambda array: (2, count // 2) + array.shape[1:]
    return pl.pallas_call(
        factor_kernel,
        out_shape=[
            jax.ShapeDtypeStruct((size, size), jnp.bfloat16),
            jax.ShapeDtypeStruct((size, size), jnp.bfloat16),
            jax.ShapeDtypeStruct((2,) + coeff.shape, jnp.bfloat16),
            jax.ShapeDtypeStruct(raw.shape, jnp.bfloat16),
        ],
        in_specs=[pl.BlockSpec(memory_space=pltpu.VMEM)] * 3,
        out_specs=[pl.BlockSpec(memory_space=pltpu.VMEM)] * 4,
        scratch_shapes=[
            pltpu.VMEM((size, size), jnp.float32),
            pltpu.VMEM((BLK, BLK), jnp.float32),
            pltpu.VMEM(slots(coeff), jnp.bfloat16),
            pltpu.VMEM(slots(raw), jnp.bfloat16),
            pltpu.SemaphoreType.DMA((2, 2, count)),
            pltpu.SemaphoreType.DMA((2, 2, count)),
            pltpu.SemaphoreType.DMA((count,)),
            pltpu.SemaphoreType.DMA((count,)),
        ],
        compiler_params=pltpu.CompilerParams(collective_id=2, has_side_effects=True),
        cost_estimate=pl.CostEstimate(flops=40 * 10 ** 9, bytes_accessed=8 * size * size, transcendentals=0),
    )(gram, coeff, raw)


GROUP = 8


def expert_kernel(high_ref, low_ref, coeff_ref, raw_ref, down_ref, other_ref, back_ref, final, answers, send, recv):
    count, capacity, width = back_ref.shape
    me = lax.axis_index("expert")
    span = GROUP * capacity
    groups = count // GROUP
    barrier = pltpu.get_barrier_semaphore()

    def greet(step, carry):
        pl.semaphore_signal(barrier, inc=1, device_id={"expert": lax.rem(me + step, count)}, device_id_type=MESH)
        return carry

    lax.fori_loop(1, count, greet, 0)
    high = high_ref[...]
    low = low_ref[...]
    for index in range(4):
        side, pick = divmod(index, 2)
        block = jnp.concatenate([coeff_ref[side, piece, pick] for piece in range(coeff_ref.shape[1])], axis=0)
        final[index] = (jnp.dot(high, block, preferred_element_type=jnp.float32)
                        + jnp.dot(low, block, preferred_element_type=jnp.float32)).astype(jnp.bfloat16)
    pl.semaphore_wait(barrier, count - 1)

    def give(target):
        return pltpu.make_async_remote_copy(
            src_ref=answers.at[target], dst_ref=back_ref.at[me], send_sem=send.at[target], recv_sem=recv.at[me],
            device_id={"expert": target}, device_id_type=MESH)

    def take(source):
        return pltpu.make_async_remote_copy(
            src_ref=back_ref.at[source], dst_ref=back_ref.at[source], send_sem=send.at[source], recv_sem=recv.at[source],
            device_id={"expert": source}, device_id_type=MESH)

    dims = (((1,), (1,)), ((), ()))

    def compute(turn, carry):
        group = lax.rem(me // GROUP + turn, groups)
        rows = raw_ref[pl.ds(pl.multiple_of(group * span, 16), span), :]
        projected = (lax.dot_general(rows, high_ref[...], dims, preferred_element_type=jnp.float32)
                     + lax.dot_general(rows, low_ref[...], dims, preferred_element_type=jnp.float32)).astype(jnp.bfloat16)
        total = jnp.zeros((span, width), jnp.float32)
        for side, rows_ref in enumerate((down_ref, other_ref)):
            gate = jnp.dot(projected, final[2 * side], preferred_element_type=jnp.float32)
            up = jnp.dot(projected, final[2 * side + 1], preferred_element_type=jnp.float32)
            hidden = (gate / (1.0 + jnp.exp(-gate)) * up).astype(jnp.bfloat16)
            total = total + jnp.dot(hidden, rows_ref[...], preferred_element_type=jnp.float32)
        for index in range(GROUP):
            target = group * GROUP + index
            value = total[index * capacity:(index + 1) * capacity].astype(jnp.bfloat16)

            @pl.when(target == me)
            def _():
                back_ref[me] = value

            @pl.when(target != me)
            def _():
                answers[target] = value
                give(target).start()
        return carry

    lax.fori_loop(0, groups, compute, 0)

    def drain(step, carry):
        take(lax.rem(me + step, count)).wait_recv()
        give(lax.rem(me + step, count)).wait_send()
        return carry

    lax.fori_loop(1, count, drain, 0)


def expert_answers(high, low, coeff, raw, down, other, count, capacity):
    rank = high.shape[0]
    width = down.shape[1]
    return pl.pallas_call(
        expert_kernel,
        out_shape=jax.ShapeDtypeStruct((count, capacity, width), jnp.bfloat16),
        in_specs=[pl.BlockSpec(memory_space=pltpu.VMEM)] * 6,
        out_specs=pl.BlockSpec(memory_space=pltpu.VMEM),
        scratch_shapes=[
            pltpu.VMEM((4, rank, rank), jnp.bfloat16),
            pltpu.VMEM((count, capacity, width), jnp.bfloat16),
            pltpu.SemaphoreType.DMA((count,)),
            pltpu.SemaphoreType.DMA((count,)),
        ],
        compiler_params=pltpu.CompilerParams(collective_id=4, has_side_effects=True),
        cost_estimate=pl.CostEstimate(flops=20 * 10 ** 9, bytes_accessed=8 * rank * rank, transcendentals=0),
    )(high, low, coeff, raw, down, other)


def transposed_dot(left, right):
    return lax.dot_general(left, right, (((0,), (0,)), ((), ())), preferred_element_type=jnp.float32)


def on_device(tokens, gate_weight, up_weight, down_weight, sketch, clusters, routes, route_weights):
    gate_rows = gate_weight[0]
    up_rows = up_weight[0]
    experts = lax.axis_size("expert")
    tensors = lax.axis_size("tensor")
    half = lax.axis_index("dp")
    sketched = jnp.dot(gate_rows, sketch[0, 0], preferred_element_type=jnp.float32) + jnp.dot(
        up_rows, sketch[0, 1], preferred_element_type=jnp.float32
    )
    rank = sketched.shape[1]

    summed = cluster_sum(sketched, clusters)

    tok_rows, width = tokens.shape
    top_count = routes.shape[1]
    capacity = tok_rows * top_count * 3 // (2 * experts)
    named = routes.T[None] == jnp.arange(experts, dtype=jnp.int32)[:, None, None]
    chosen = jnp.any(named, axis=1)
    shares = jnp.sum(jnp.where(named, route_weights.T[None], 0.0), axis=1)
    token_index = jnp.arange(tok_rows)
    earlier = (token_index[:, None] < token_index[None, :]).astype(jnp.bfloat16)
    place = jnp.dot(chosen.astype(jnp.bfloat16), earlier, preferred_element_type=jnp.float32).astype(jnp.int32)
    holds = chosen[:, None, :] & (place[:, None, :] == jnp.arange(capacity, dtype=jnp.int32)[None, :, None])
    select = holds.astype(jnp.bfloat16).reshape(experts * capacity, tok_rows)
    outgoing = jnp.dot(select, tokens, preferred_element_type=jnp.float32).astype(jnp.bfloat16)
    outgoing = outgoing.reshape(experts, capacity, width)

    columns = lax.dynamic_slice_in_dim(summed, half * (rank // 2), rank // 2, 1)
    gram = transposed_dot(summed, columns).reshape(tensors, rank // tensors, rank // 2)
    gram, down_other, coeff, raw = gram_sum(gram, down_weight[0], outgoing, summed, gate_rows, up_rows)
    high, low, coeff, raw = inverse_and_sums(gram, coeff, raw)
    returned = expert_answers(
        high, low, coeff, raw.reshape(experts * capacity, rank),
        down_weight[0], down_other, experts, capacity)
    returned = returned.reshape(experts * capacity, width)
    mixing = jnp.where(holds, shares[:, None, :], 0.0).reshape(experts * capacity, tok_rows)
    high = mixing.astype(jnp.bfloat16)
    low = (mixing - high.astype(jnp.float32)).astype(jnp.bfloat16)
    return (transposed_dot(high, returned) + transposed_dot(low, returned)).astype(jnp.bfloat16)


def solution(mesh):
    return jax.shard_map(
        on_device,
        mesh=mesh,
        in_specs=(
            P(("expert", "dp"), "tensor"),
            P("expert", "tensor", "dp"),
            P("expert", "tensor", "dp"),
            P("expert", "dp", "tensor"),
            P("expert", None, "dp", None),
            P(),
            P(("expert", "dp"), None),
            P(("expert", "dp"), None),
        ),
        out_specs=P(("expert", "dp"), "tensor"),
        check_vma=False,
    )
```

```python
import jax
import jax.numpy as jnp
from jax import lax
from jax.experimental import pallas as pl
from jax.experimental.pallas import tpu as pltpu
from jax.sharding import PartitionSpec as P

MESH = pl.DeviceIdType.MESH
HIGHEST = lax.Precision.HIGHEST
BLK = 128


def factor_block(tiles, serve):
    lane = lax.broadcasted_iota(jnp.int32, (8, BLK), 1)
    sub = lax.broadcasted_iota(jnp.int32, (8, BLK), 0)
    n = BLK // 8
    tiles = list(tiles)
    for k in range(0, BLK, 2):
        t, r = divmod(k, 8)
        cur = tiles[t]
        col1 = jnp.broadcast_to(cur[:, k:k + 1], (8, BLK))
        col2 = jnp.broadcast_to(cur[:, k + 1:k + 2], (8, BLK))
        a = col1[r:r + 1, :]
        b = col1[r + 1:r + 2, :]
        c = col2[r + 1:r + 2, :]
        ra = 1.0 / a
        rc = a / (a * c - b * b)
        first, second = lane == k, lane == k + 1
        both = jnp.logical_or(first, second)
        row1 = jnp.where(first[:1], 1.0, jnp.where(second[:1], 0.0, cur[r:r + 1, :]))
        row2 = jnp.where(both[:1], 0.0, cur[r + 1:r + 2, :]) - (b * ra) * row1
        row2 = jnp.where(second[:1], 1.0, row2)
        v2 = rc * row2
        v1 = ra * row1 - (b * ra) * v2
        for i in range(t, n):
            old = tiles[i]
            if i == t:
                new = jnp.where(both, 0.0, old) - col1 * v1 - col2 * v2
                new = jnp.where(sub > r + 1, new, old)
                new = jnp.where(sub == r, row1 * jnp.sqrt(ra), new)
                new = jnp.where(sub == r + 1, row2 * jnp.sqrt(rc), new)
            else:
                c1 = jnp.broadcast_to(old[:, k:k + 1], (8, BLK))
                c2 = jnp.broadcast_to(old[:, k + 1:k + 2], (8, BLK))
                new = jnp.where(both, 0.0, old) - c1 * v1 - c2 * v2
            tiles[i] = new
        if k % 32 == 30:
            serve(k // 32)
    return [jnp.where(lane <= sub + 8 * i, tiles[i], 0.0) for i in range(n)]

def eliminate(out_ref, inv_ref, serve):
    size = out_ref.shape[0]
    steps = size // BLK

    def step(j, carry):
        at = pl.multiple_of(j * BLK, BLK)
        tiles = [out_ref[pl.ds(pl.multiple_of(at + 8 * i, 8), 8), pl.ds(at, BLK)] for i in range(BLK // 8)]
        for i, tile in enumerate(factor_block(tiles, lambda turn: serve(turn % 2, 2 * j + turn // 2))):
            inv_ref[8 * i:8 * i + 8, :] = tile
        inv = inv_ref[...]
        rows = lax.broadcasted_iota(jnp.int32, (BLK, BLK), 0)
        cols = lax.broadcasted_iota(jnp.int32, (BLK, BLK), 1)
        eye = jnp.where(rows == cols, 1.0, 0.0)
        out_ref[pl.ds(at, BLK), pl.ds(at, BLK)] = eye
        full = jnp.dot(inv, out_ref[pl.ds(at, BLK), :], precision=HIGHEST, preferred_element_type=jnp.float32)
        column = lax.broadcasted_iota(jnp.int32, (BLK, size), 1)
        later = jnp.where(column >= at + BLK, full, 0.0)
        out_ref[pl.ds(at, BLK), :] = full
        column = lax.broadcasted_iota(jnp.int32, (size, size), 1)
        row = lax.broadcasted_iota(jnp.int32, (size, size), 0)
        zero = (column >= at) & (column < at + BLK) & (row >= at + BLK)
        out_ref[...] = jnp.where(zero, 0.0, out_ref[...]) - lax.dot_general(
            later, full, (((0,), (0,)), ((), ())), precision=HIGHEST, preferred_element_type=jnp.float32)
        return carry

    lax.fori_loop(0, steps, step, 0)
    row = lax.broadcasted_iota(jnp.int32, (size, size), 0)
    column = lax.broadcasted_iota(jnp.int32, (size, size), 1)
    out_ref[...] = jnp.where(column <= row, out_ref[...], 0.0)

REACH = 3
CUTS = 7


def cluster_kernel(part_ref, cluster_ref, out_ref, stage, got, own, plus, minus, acc,
                   dp_send, dp_recv, up_send, up_recv, low_send, low_recv, fin_send, fin_recv):
    count = lax.axis_size("expert")
    me = lax.axis_index("expert")
    half = lax.axis_index("dp")
    sibling = {"dp": 1 - half}
    after = {"expert": lax.rem(me + 1, count)}
    before = {"expert": lax.rem(me + count - 1, count)}
    part = part_ref.shape[0] // 2
    size = part // CUTS
    mine = cluster_ref[me]

    def share(step):
        other = me + step
        inside = jnp.logical_and(other >= 0, other < count)
        same = cluster_ref[lax.rem(other + count, count)] == mine
        return jnp.where(jnp.logical_and(inside, same), 1.0, 0.0).astype(jnp.float32)

    barrier = pltpu.get_barrier_semaphore()
    for device in (sibling, after, before):
        pl.semaphore_signal(barrier, inc=1, device_id=device, device_id_type=MESH)

    def rows(side, cut):
        return pl.ds(pl.multiple_of(side * part + cut * size, 16), size)

    def remote(src, dst, send, recv, device):
        return pltpu.make_async_remote_copy(
            src_ref=src, dst_ref=dst, send_sem=send, recv_sem=recv, device_id=device, device_id_type=MESH)

    def swap(cut):
        return remote(stage.at[cut], got.at[cut], dp_send.at[cut], dp_recv.at[cut], sibling)

    def ahead(hop, cut):
        source = own.at[cut] if hop == 0 else plus.at[hop - 1, cut]
        return remote(source, plus.at[hop, cut], up_send.at[hop, cut], up_recv.at[hop, cut], after)

    def back(hop, cut):
        source = own.at[cut] if hop == 0 else minus.at[hop - 1, cut]
        return remote(source, minus.at[hop, cut], low_send.at[hop, cut], low_recv.at[hop, cut], before)

    def finish(cut):
        place = out_ref.at[rows(half, cut)]
        return remote(place, place, fin_send.at[cut], fin_recv.at[cut], sibling)

    for cut in range(CUTS):
        stage[cut] = part_ref[rows(1 - half, cut), :].astype(jnp.bfloat16)
    pl.semaphore_wait(barrier, 3)
    for cut in range(CUTS):
        swap(cut).start()
    for cut in range(CUTS):
        swap(cut).wait_recv()
        value = (part_ref[rows(half, cut), :] + got[cut].astype(jnp.float32)).astype(jnp.bfloat16)
        own[cut] = value
        ahead(0, cut).start()
        back(0, cut).start()
        acc[cut] = value.astype(jnp.float32)
    for hop in range(REACH):
        for cut in range(CUTS):
            ahead(hop, cut).wait_recv()
            if hop < REACH - 1:
                ahead(hop + 1, cut).start()
            back(hop, cut).wait_recv()
            if hop < REACH - 1:
                back(hop + 1, cut).start()
            total = acc[cut] + share(-1 - hop) * plus[hop, cut].astype(jnp.float32)
            total = total + share(hop + 1) * minus[hop, cut].astype(jnp.float32)
            if hop < REACH - 1:
                acc[cut] = total
            else:
                out_ref[rows(half, cut), :] = total.astype(jnp.bfloat16)
                finish(cut).start()
    for cut in range(CUTS):
        finish(cut).wait_recv()
        finish(cut).wait_send()
        swap(cut).wait_send()
        for hop in range(REACH):
            ahead(hop, cut).wait_send()
            back(hop, cut).wait_send()


def cluster_sum(sketched, clusters):
    rows, rank = sketched.shape
    size = rows // 2 // CUTS
    return pl.pallas_call(
        cluster_kernel,
        out_shape=jax.ShapeDtypeStruct((rows, rank), jnp.bfloat16),
        in_specs=[pl.BlockSpec(memory_space=pltpu.VMEM), pl.BlockSpec(memory_space=pltpu.SMEM)],
        out_specs=pl.BlockSpec(memory_space=pltpu.VMEM),
        scratch_shapes=[
            pltpu.VMEM((CUTS, size, rank), jnp.bfloat16),
            pltpu.VMEM((CUTS, size, rank), jnp.bfloat16),
            pltpu.VMEM((CUTS, size, rank), jnp.bfloat16),
            pltpu.VMEM((REACH, CUTS, size, rank), jnp.bfloat16),
            pltpu.VMEM((REACH, CUTS, size, rank), jnp.bfloat16),
            pltpu.VMEM((CUTS, size, rank), jnp.float32),
            pltpu.SemaphoreType.DMA((CUTS,)),
            pltpu.SemaphoreType.DMA((CUTS,)),
            pltpu.SemaphoreType.DMA((REACH, CUTS)),
            pltpu.SemaphoreType.DMA((REACH, CUTS)),
            pltpu.SemaphoreType.DMA((REACH, CUTS)),
            pltpu.SemaphoreType.DMA((REACH, CUTS)),
            pltpu.SemaphoreType.DMA((CUTS,)),
            pltpu.SemaphoreType.DMA((CUTS,)),
        ],
        compiler_params=pltpu.CompilerParams(collective_id=3, has_side_effects=True),
        cost_estimate=pl.CostEstimate(flops=10 ** 10, bytes_accessed=8 * rows * rank, transcendentals=0),
    )(sketched, clusters)


GROUP = 8


def whole_kernel(part_ref, down_ref, send_ref, sum_ref, gate_ref, up_ref, back_ref,
                 arrive, pieces, landed, other, coeff_part, raw_part, work, inv_ref, coeff_slot, raw_slot,
                 high_ref, low_ref, coeff_all, raw_all, final, answers,
                 rs_send, rs_recv, ag_send, ag_recv, hand_send, hand_recv, down_send, down_recv, tok_send, tok_recv,
                 ring_send, ring_recv, share_send, share_recv, ans_send, ans_recv):
    me = lax.axis_index("tensor")
    half = lax.axis_index("dp")
    expert = lax.axis_index("expert")
    experts, capacity, depth = send_ref.shape
    count, height, width = part_ref.shape
    longer = count // 2
    reach = (longer, longer - 1)
    sibling = {"dp": 1 - half}
    after = {"tensor": lax.rem(me + 1, count)}
    before = {"tensor": lax.rem(me + count - 1, count)}
    parts, slots = (coeff_part, raw_part), (coeff_slot, raw_slot)
    barrier = pltpu.get_barrier_semaphore()
    for step in range(1, count):
        pl.semaphore_signal(barrier, inc=1, device_id={"tensor": lax.rem(me + step, count)}, device_id_type=MESH)
    pl.semaphore_signal(barrier, inc=1, device_id=sibling, device_id_type=MESH)

    def greet(step, carry):
        pl.semaphore_signal(barrier, inc=1, device_id={"expert": lax.rem(expert + step, experts)}, device_id_type=MESH)
        return carry

    lax.fori_loop(1, experts, greet, 0)
    pl.semaphore_wait(barrier, count + experts - 1)

    def remote(src, dst, send, recv, device):
        return pltpu.make_async_remote_copy(
            src_ref=src, dst_ref=dst, send_sem=send, recv_sem=recv, device_id=device, device_id_type=MESH)

    def scatter(step):
        peer = lax.rem(me + step, count)
        return remote(part_ref.at[peer], arrive.at[step], rs_send.at[step], rs_recv.at[step], {"tensor": peer})

    def spread(step):
        mine = pieces.at[half * count + me]
        return remote(mine, mine, ag_send.at[step], ag_recv.at[step], {"tensor": lax.rem(me + step, count)})

    def hand(step):
        piece = pieces.at[half * count + lax.rem(me + count - step, count)]
        return remote(piece, piece, hand_send.at[step], hand_recv.at[step], sibling)

    def route(step):
        peer = lax.rem(expert + step, experts)
        return remote(send_ref.at[peer], landed.at[expert], tok_send.at[peer], tok_recv.at[expert], {"expert": peer})

    def landing(source):
        return remote(send_ref.at[source], landed.at[source], tok_send.at[source], tok_recv.at[source], {"expert": source})

    def upward(kind, side):
        return kind == side

    def chunk(kind, side, distance):
        return lax.rem(me + (distance if upward(kind, side) else count - distance), count)

    def place(kind, index):
        return coeff_all.at[0, index] if kind == 0 else raw_all.at[index]

    def ring(src, dst, kind, side, turn):
        return remote(src, dst, ring_send.at[kind, side, turn], ring_recv.at[kind, side, turn],
                      after if upward(kind, side) else before)

    def first(kind, side):
        return ring(parts[kind].at[chunk(kind, side, reach[side])], slots[kind].at[side, 0], kind, side, 0)

    def add_on(kind, side, turn):
        return ring(slots[kind].at[side, turn - 1], slots[kind].at[side, turn], kind, side, turn)

    def pass_on(kind, side, hop):
        here = place(kind, lax.rem(me + (count - hop if upward(kind, side) else hop), count))
        return ring(here, here, kind, side, longer + hop)

    def share(index):
        return remote(coeff_all.at[0, index], coeff_all.at[1, index], share_send.at[index], share_recv.at[index], sibling)

    def serve(kind, turn):
        for side in range(2):
            @pl.when(turn < reach[side])
            def _():
                slot = slots[kind].at[side, turn]
                ring(slot, slot, kind, side, turn).wait_recv()

            @pl.when(turn < reach[side] - 1)
            def _():
                value = parts[kind][chunk(kind, side, reach[side] - 1 - turn)].astype(jnp.float32)
                slots[kind][side, turn] = (slots[kind][side, turn].astype(jnp.float32) + value).astype(jnp.bfloat16)
                add_on(kind, side, turn + 1).start()

        @pl.when(turn == longer - 1)
        def _():
            value = parts[kind][me].astype(jnp.float32) + slots[kind][0, longer - 1].astype(jnp.float32)
            value = value + slots[kind][1, longer - 2].astype(jnp.float32)
            place(kind, me)[...] = value.astype(jnp.bfloat16)
            for side in range(2):
                pass_on(kind, side, 0).start()
            if kind == 0:
                share(me).start()

        hop = turn - longer
        for side in range(2):
            index = lax.rem(me + (2 * count - 1 - hop if upward(kind, side) else hop + 1), count)

            @pl.when((hop >= 0) & (hop < reach[side]))
            def _():
                ring(place(kind, index), place(kind, index), kind, side, turn).wait_recv()
                if kind == 0:
                    share(index).start()

            @pl.when((hop >= 0) & (hop < reach[side] - 1))
            def _():
                pass_on(kind, side, hop + 1).start()

    down = remote(down_ref, other, down_send, down_recv, sibling)
    order = [4, 3, 5, 2, 6, 1, 7]
    for step in order:
        scatter(step).start()

    def route_all(step, carry):
        route(step).start()
        return carry

    lax.fori_loop(1, experts, route_all, 0)
    down.start()
    landed[expert] = send_ref[expert]
    turned = (((0,), (0,)), ((), ()))
    for pick, rows_ref in enumerate((gate_ref, up_ref)):
        block = lax.dot_general(sum_ref[...], rows_ref[...], turned, preferred_element_type=jnp.float32)
        for piece in range(count):
            coeff_part[piece, pick] = block[piece * height:(piece + 1) * height].astype(jnp.bfloat16)
    total = part_ref[me]
    for step in reversed(order):
        scatter(step).wait_recv()
        total = total + arrive[step]
    pieces[half * count + me] = total
    for step in order:
        spread(step).start()
    hand(0).start()
    for side in range(2):
        first(0, side).start()
    for step in reversed(order):
        spread(step).wait_recv()
        hand(step).start()
    for step in range(count):
        hand(step).wait_recv()
    for side in range(2):
        for piece in range(count):
            work[piece * height:(piece + 1) * height, side * width:(side + 1) * width] = pieces[side * count + piece]

    def settle(step, carry):
        landing(lax.rem(expert + step, experts)).wait_recv()
        return carry

    lax.fori_loop(1, experts, settle, 0)
    group = raw_part.shape[1] // capacity

    def project(index, carry):
        rows = jnp.concatenate([landed[index * group + item].astype(jnp.float32) for item in range(group)], axis=0)
        raw_part[index] = jnp.dot(
            rows.astype(jnp.bfloat16), sum_ref[...], preferred_element_type=jnp.float32).astype(jnp.bfloat16)
        return carry

    lax.fori_loop(0, experts // group, project, 0)
    for side in range(2):
        first(1, side).start()
    eliminate(work, inv_ref, serve)
    high = work[...].astype(jnp.bfloat16)
    high_ref[...] = high
    low_ref[...] = (work[...] - high.astype(jnp.float32)).astype(jnp.bfloat16)

    def gathered(index, carry):
        share(index).wait_recv()
        return carry

    lax.fori_loop(0, count, gathered, 0)
    down.wait_recv()
    low = low_ref[...]
    for index in range(4):
        side, pick = divmod(index, 2)
        block = jnp.concatenate([coeff_all[side, piece, pick] for piece in range(count)], axis=0)
        final[index] = (jnp.dot(high, block, preferred_element_type=jnp.float32)
                        + jnp.dot(low, block, preferred_element_type=jnp.float32)).astype(jnp.bfloat16)

    def give(target):
        return remote(answers.at[target], back_ref.at[expert], ans_send.at[target], ans_recv.at[expert], {"expert": target})

    def take(source):
        return remote(back_ref.at[source], back_ref.at[source], ans_send.at[source], ans_recv.at[source], {"expert": source})

    dims = (((1,), (1,)), ((), ()))
    groups = experts // GROUP
    span = GROUP * capacity
    each = span // raw_all.shape[1]

    def compute(turn, carry):
        block = lax.rem(expert // GROUP + turn, groups)
        rows = jnp.concatenate([raw_all[block * each + item] for item in range(each)], axis=0)
        projected = (lax.dot_general(rows, high_ref[...], dims, preferred_element_type=jnp.float32)
                     + lax.dot_general(rows, low_ref[...], dims, preferred_element_type=jnp.float32)).astype(jnp.bfloat16)
        result = jnp.zeros((span, depth), jnp.float32)
        for side, rows_ref in enumerate((down_ref, other)):
            gate = jnp.dot(projected, final[2 * side], preferred_element_type=jnp.float32)
            up = jnp.dot(projected, final[2 * side + 1], preferred_element_type=jnp.float32)
            hidden = (gate / (1.0 + jnp.exp(-gate)) * up).astype(jnp.bfloat16)
            result = result + jnp.dot(hidden, rows_ref[...], preferred_element_type=jnp.float32)
        for index in range(GROUP):
            target = block * GROUP + index
            value = result[index * capacity:(index + 1) * capacity].astype(jnp.bfloat16)

            @pl.when(target == expert)
            def _():
                back_ref[expert] = value

            @pl.when(target != expert)
            def _():
                answers[target] = value
                give(target).start()
        return carry

    lax.fori_loop(0, groups, compute, 0)
    for step in order:
        scatter(step).wait_send()
        spread(step).wait_send()
    for step in range(count):
        hand(step).wait_send()
        share(step).wait_send()
    down.wait_send()
    for kind in range(2):
        for side in range(2):
            first(kind, side).wait_send()
            for turn in range(1, reach[side]):
                add_on(kind, side, turn).wait_send()
            for hop in range(reach[side]):
                pass_on(kind, side, hop).wait_send()

    def drain(step, carry):
        route(step).wait_send()
        take(lax.rem(expert + step, experts)).wait_recv()
        give(lax.rem(expert + step, experts)).wait_send()
        return carry

    lax.fori_loop(1, experts, drain, 0)


def expert_answers(part, down, outgoing, summed, gate, up):
    count, height, width = part.shape
    size = count * height
    experts, capacity, depth = outgoing.shape
    hidden = gate.shape[1]
    rows = experts * capacity // count
    low, full = jnp.bfloat16, jnp.float32
    dma = pltpu.SemaphoreType.DMA
    return pl.pallas_call(
        whole_kernel,
        out_shape=jax.ShapeDtypeStruct(outgoing.shape, low),
        in_specs=[pl.BlockSpec(memory_space=pltpu.VMEM)] * 6,
        out_specs=pl.BlockSpec(memory_space=pltpu.VMEM),
        scratch_shapes=[
            pltpu.VMEM((count, height, width), full),
            pltpu.VMEM((2 * count, height, width), full),
            pltpu.VMEM((experts, capacity, depth), low),
            pltpu.VMEM(down.shape, low),
            pltpu.VMEM((count, 2, height, hidden), low),
            pltpu.VMEM((count, rows, size), low),
            pltpu.VMEM((size, size), full),
            pltpu.VMEM((BLK, BLK), full),
            pltpu.VMEM((2, count // 2, 2, height, hidden), low),
            pltpu.VMEM((2, count // 2, rows, size), low),
            pltpu.VMEM((size, size), low),
            pltpu.VMEM((size, size), low),
            pltpu.VMEM((2, count, 2, height, hidden), low),
            pltpu.VMEM((count, rows, size), low),
            pltpu.VMEM((4, size, hidden), low),
            pltpu.VMEM((experts, capacity, depth), low),
        ] + [dma((count,))] * 6 + [dma] * 2 + [dma((experts,))] * 2 + [dma((2, 2, count))] * 2 + [dma((count,))] * 2
        + [dma((experts,))] * 2,
        compiler_params=pltpu.CompilerParams(collective_id=1, has_side_effects=True),
        cost_estimate=pl.CostEstimate(flops=10 ** 11, bytes_accessed=8 * size * size, transcendentals=0),
    )(part, down, outgoing, summed, gate, up)


def transposed_dot(left, right):
    return lax.dot_general(left, right, (((0,), (0,)), ((), ())), preferred_element_type=jnp.float32)


def on_device(tokens, gate_weight, up_weight, down_weight, sketch, clusters, routes, route_weights):
    gate_rows = gate_weight[0]
    up_rows = up_weight[0]
    experts = lax.axis_size("expert")
    tensors = lax.axis_size("tensor")
    half = lax.axis_index("dp")
    sketched = jnp.dot(gate_rows, sketch[0, 0], preferred_element_type=jnp.float32) + jnp.dot(
        up_rows, sketch[0, 1], preferred_element_type=jnp.float32
    )
    rank = sketched.shape[1]

    summed = cluster_sum(sketched, clusters)

    tok_rows, width = tokens.shape
    top_count = routes.shape[1]
    capacity = tok_rows * top_count * 3 // (2 * experts)
    named = routes.T[None] == jnp.arange(experts, dtype=jnp.int32)[:, None, None]
    chosen = jnp.any(named, axis=1)
    shares = jnp.sum(jnp.where(named, route_weights.T[None], 0.0), axis=1)
    token_index = jnp.arange(tok_rows)
    earlier = (token_index[:, None] < token_index[None, :]).astype(jnp.bfloat16)
    place = jnp.dot(chosen.astype(jnp.bfloat16), earlier, preferred_element_type=jnp.float32).astype(jnp.int32)
    holds = chosen[:, None, :] & (place[:, None, :] == jnp.arange(capacity, dtype=jnp.int32)[None, :, None])
    select = holds.astype(jnp.bfloat16).reshape(experts * capacity, tok_rows)
    outgoing = jnp.dot(select, tokens, preferred_element_type=jnp.float32).astype(jnp.bfloat16)
    outgoing = outgoing.reshape(experts, capacity, width)

    columns = lax.dynamic_slice_in_dim(summed, half * (rank // 2), rank // 2, 1)
    gram = transposed_dot(summed, columns).reshape(tensors, rank // tensors, rank // 2)
    returned = expert_answers(gram, down_weight[0], outgoing, summed, gate_rows, up_rows)
    returned = returned.reshape(experts * capacity, width)
    mixing = jnp.where(holds, shares[:, None, :], 0.0).reshape(experts * capacity, tok_rows)
    high = mixing.astype(jnp.bfloat16)
    low = (mixing - high.astype(jnp.float32)).astype(jnp.bfloat16)
    return (transposed_dot(high, returned) + transposed_dot(low, returned)).astype(jnp.bfloat16)


def solution(mesh):
    return jax.shard_map(
        on_device,
        mesh=mesh,
        in_specs=(
            P(("expert", "dp"), "tensor"),
            P("expert", "tensor", "dp"),
            P("expert", "tensor", "dp"),
            P("expert", "dp", "tensor"),
            P("expert", None, "dp", None),
            P(),
            P(("expert", "dp"), None),
            P(("expert", "dp"), None),
        ),
        out_specs=P(("expert", "dp"), "tensor"),
        check_vma=False,
    )
```

```python
import jax
import jax.numpy as jnp
from jax import lax
from jax.experimental import pallas as pl
from jax.experimental.pallas import tpu as pltpu
from jax.sharding import PartitionSpec as P

MESH = pl.DeviceIdType.MESH
HIGHEST = lax.Precision.HIGHEST
BLK = 128


def factor_block(tiles, serve):
    lane = lax.broadcasted_iota(jnp.int32, (8, BLK), 1)
    sub = lax.broadcasted_iota(jnp.int32, (8, BLK), 0)
    n = BLK // 8
    tiles = list(tiles)
    for k in range(0, BLK, 2):
        t, r = divmod(k, 8)
        cur = tiles[t]
        col1 = jnp.broadcast_to(cur[:, k:k + 1], (8, BLK))
        col2 = jnp.broadcast_to(cur[:, k + 1:k + 2], (8, BLK))
        a = col1[r:r + 1, :]
        b = col1[r + 1:r + 2, :]
        c = col2[r + 1:r + 2, :]
        ra = 1.0 / a
        rc = a / (a * c - b * b)
        first, second = lane == k, lane == k + 1
        both = jnp.logical_or(first, second)
        row1 = jnp.where(first[:1], 1.0, jnp.where(second[:1], 0.0, cur[r:r + 1, :]))
        row2 = jnp.where(both[:1], 0.0, cur[r + 1:r + 2, :]) - (b * ra) * row1
        row2 = jnp.where(second[:1], 1.0, row2)
        v2 = rc * row2
        v1 = ra * row1 - (b * ra) * v2
        for i in range(t, n):
            old = tiles[i]
            if i == t:
                new = jnp.where(both, 0.0, old) - col1 * v1 - col2 * v2
                new = jnp.where(sub > r + 1, new, old)
                new = jnp.where(sub == r, row1 * jnp.sqrt(ra), new)
                new = jnp.where(sub == r + 1, row2 * jnp.sqrt(rc), new)
            else:
                c1 = jnp.broadcast_to(old[:, k:k + 1], (8, BLK))
                c2 = jnp.broadcast_to(old[:, k + 1:k + 2], (8, BLK))
                new = jnp.where(both, 0.0, old) - c1 * v1 - c2 * v2
            tiles[i] = new
        if k % 32 == 30:
            serve(k // 32)
    return [jnp.where(lane <= sub + 8 * i, tiles[i], 0.0) for i in range(n)]

def eliminate(out_ref, inv_ref, serve):
    size = out_ref.shape[0]
    steps = size // BLK

    def step(j, carry):
        at = pl.multiple_of(j * BLK, BLK)
        tiles = [out_ref[pl.ds(pl.multiple_of(at + 8 * i, 8), 8), pl.ds(at, BLK)] for i in range(BLK // 8)]
        for i, tile in enumerate(factor_block(tiles, lambda turn: serve(turn % 2, 2 * j + turn // 2))):
            inv_ref[8 * i:8 * i + 8, :] = tile
        inv = inv_ref[...]
        rows = lax.broadcasted_iota(jnp.int32, (BLK, BLK), 0)
        cols = lax.broadcasted_iota(jnp.int32, (BLK, BLK), 1)
        eye = jnp.where(rows == cols, 1.0, 0.0)
        out_ref[pl.ds(at, BLK), pl.ds(at, BLK)] = eye
        full = jnp.dot(inv, out_ref[pl.ds(at, BLK), :], precision=HIGHEST, preferred_element_type=jnp.float32)
        column = lax.broadcasted_iota(jnp.int32, (BLK, size), 1)
        later = jnp.where(column >= at + BLK, full, 0.0)
        out_ref[pl.ds(at, BLK), :] = full
        column = lax.broadcasted_iota(jnp.int32, (size, size), 1)
        row = lax.broadcasted_iota(jnp.int32, (size, size), 0)
        zero = (column >= at) & (column < at + BLK) & (row >= at + BLK)
        out_ref[...] = jnp.where(zero, 0.0, out_ref[...]) - lax.dot_general(
            later, full, (((0,), (0,)), ((), ())), precision=HIGHEST, preferred_element_type=jnp.float32)
        return carry

    lax.fori_loop(0, steps, step, 0)
    row = lax.broadcasted_iota(jnp.int32, (size, size), 0)
    column = lax.broadcasted_iota(jnp.int32, (size, size), 1)
    out_ref[...] = jnp.where(column <= row, out_ref[...], 0.0)

REACH = 3
CUTS = 7


def cluster_kernel(part_ref, cluster_ref, out_ref, stage, got, own, plus, minus, acc,
                   dp_send, dp_recv, up_send, up_recv, low_send, low_recv, fin_send, fin_recv):
    count = lax.axis_size("expert")
    me = lax.axis_index("expert")
    half = lax.axis_index("dp")
    sibling = {"dp": 1 - half}
    after = {"expert": lax.rem(me + 1, count)}
    before = {"expert": lax.rem(me + count - 1, count)}
    part = part_ref.shape[0] // 2
    size = part // CUTS
    mine = cluster_ref[me]

    def share(step):
        other = me + step
        inside = jnp.logical_and(other >= 0, other < count)
        same = cluster_ref[lax.rem(other + count, count)] == mine
        return jnp.where(jnp.logical_and(inside, same), 1.0, 0.0).astype(jnp.float32)

    barrier = pltpu.get_barrier_semaphore()
    for device in (sibling, after, before):
        pl.semaphore_signal(barrier, inc=1, device_id=device, device_id_type=MESH)

    def rows(side, cut):
        return pl.ds(pl.multiple_of(side * part + cut * size, 16), size)

    def remote(src, dst, send, recv, device):
        return pltpu.make_async_remote_copy(
            src_ref=src, dst_ref=dst, send_sem=send, recv_sem=recv, device_id=device, device_id_type=MESH)

    def swap(cut):
        return remote(stage.at[cut], got.at[cut], dp_send.at[cut], dp_recv.at[cut], sibling)

    def ahead(hop, cut):
        source = own.at[cut] if hop == 0 else plus.at[hop - 1, cut]
        return remote(source, plus.at[hop, cut], up_send.at[hop, cut], up_recv.at[hop, cut], after)

    def back(hop, cut):
        source = own.at[cut] if hop == 0 else minus.at[hop - 1, cut]
        return remote(source, minus.at[hop, cut], low_send.at[hop, cut], low_recv.at[hop, cut], before)

    def finish(cut):
        place = out_ref.at[rows(half, cut)]
        return remote(place, place, fin_send.at[cut], fin_recv.at[cut], sibling)

    for cut in range(CUTS):
        stage[cut] = part_ref[rows(1 - half, cut), :].astype(jnp.bfloat16)
    pl.semaphore_wait(barrier, 3)
    for cut in range(CUTS):
        swap(cut).start()
    for cut in range(CUTS):
        swap(cut).wait_recv()
        value = (part_ref[rows(half, cut), :] + got[cut].astype(jnp.float32)).astype(jnp.bfloat16)
        own[cut] = value
        ahead(0, cut).start()
        back(0, cut).start()
        acc[cut] = value.astype(jnp.float32)
    for hop in range(REACH):
        for cut in range(CUTS):
            ahead(hop, cut).wait_recv()
            if hop < REACH - 1:
                ahead(hop + 1, cut).start()
            back(hop, cut).wait_recv()
            if hop < REACH - 1:
                back(hop + 1, cut).start()
            total = acc[cut] + share(-1 - hop) * plus[hop, cut].astype(jnp.float32)
            total = total + share(hop + 1) * minus[hop, cut].astype(jnp.float32)
            if hop < REACH - 1:
                acc[cut] = total
            else:
                out_ref[rows(half, cut), :] = total.astype(jnp.bfloat16)
                finish(cut).start()
    for cut in range(CUTS):
        finish(cut).wait_recv()
        finish(cut).wait_send()
        swap(cut).wait_send()
        for hop in range(REACH):
            ahead(hop, cut).wait_send()
            back(hop, cut).wait_send()


def cluster_sum(sketched, clusters):
    rows, rank = sketched.shape
    size = rows // 2 // CUTS
    return pl.pallas_call(
        cluster_kernel,
        out_shape=jax.ShapeDtypeStruct((rows, rank), jnp.bfloat16),
        in_specs=[pl.BlockSpec(memory_space=pltpu.VMEM), pl.BlockSpec(memory_space=pltpu.SMEM)],
        out_specs=pl.BlockSpec(memory_space=pltpu.VMEM),
        scratch_shapes=[
            pltpu.VMEM((CUTS, size, rank), jnp.bfloat16),
            pltpu.VMEM((CUTS, size, rank), jnp.bfloat16),
            pltpu.VMEM((CUTS, size, rank), jnp.bfloat16),
            pltpu.VMEM((REACH, CUTS, size, rank), jnp.bfloat16),
            pltpu.VMEM((REACH, CUTS, size, rank), jnp.bfloat16),
            pltpu.VMEM((CUTS, size, rank), jnp.float32),
            pltpu.SemaphoreType.DMA((CUTS,)),
            pltpu.SemaphoreType.DMA((CUTS,)),
            pltpu.SemaphoreType.DMA((REACH, CUTS)),
            pltpu.SemaphoreType.DMA((REACH, CUTS)),
            pltpu.SemaphoreType.DMA((REACH, CUTS)),
            pltpu.SemaphoreType.DMA((REACH, CUTS)),
            pltpu.SemaphoreType.DMA((CUTS,)),
            pltpu.SemaphoreType.DMA((CUTS,)),
        ],
        compiler_params=pltpu.CompilerParams(collective_id=3, has_side_effects=True),
        cost_estimate=pl.CostEstimate(flops=10 ** 10, bytes_accessed=8 * rows * rank, transcendentals=0),
    )(sketched, clusters)


GROUP = 8


def whole_kernel(part_ref, down_ref, send_ref, sum_ref, gate_ref, up_ref, back_ref,
                 arrive, pieces, landed, other, coeff_part, raw_part, work, inv_ref, coeff_slot, raw_slot,
                 high_ref, low_ref, coeff_all, raw_all, final, answers,
                 rs_send, rs_recv, ag_send, ag_recv, hand_send, hand_recv, down_send, down_recv, tok_send, tok_recv,
                 ring_send, ring_recv, share_send, share_recv, ans_send, ans_recv):
    me = lax.axis_index("tensor")
    half = lax.axis_index("dp")
    expert = lax.axis_index("expert")
    experts, capacity, depth = send_ref.shape
    count, height, width = part_ref.shape
    longer = count // 2
    reach = (longer, longer - 1)
    sibling = {"dp": 1 - half}
    after = {"tensor": lax.rem(me + 1, count)}
    before = {"tensor": lax.rem(me + count - 1, count)}
    parts, slots = (coeff_part, raw_part), (coeff_slot, raw_slot)
    barrier = pltpu.get_barrier_semaphore()
    for step in range(1, count):
        pl.semaphore_signal(barrier, inc=1, device_id={"tensor": lax.rem(me + step, count)}, device_id_type=MESH)
    pl.semaphore_signal(barrier, inc=1, device_id=sibling, device_id_type=MESH)

    def greet(step, carry):
        pl.semaphore_signal(barrier, inc=1, device_id={"expert": lax.rem(expert + step, experts)}, device_id_type=MESH)
        return carry

    lax.fori_loop(1, experts, greet, 0)
    pl.semaphore_wait(barrier, count + experts - 1)

    def remote(src, dst, send, recv, device):
        return pltpu.make_async_remote_copy(
            src_ref=src, dst_ref=dst, send_sem=send, recv_sem=recv, device_id=device, device_id_type=MESH)

    def scatter(step):
        peer = lax.rem(me + step, count)
        return remote(part_ref.at[peer], arrive.at[step], rs_send.at[step], rs_recv.at[step], {"tensor": peer})

    def spread(step):
        mine = pieces.at[half * count + me]
        return remote(mine, mine, ag_send.at[step], ag_recv.at[step], {"tensor": lax.rem(me + step, count)})

    def hand(step):
        piece = pieces.at[half * count + lax.rem(me + count - step, count)]
        return remote(piece, piece, hand_send.at[step], hand_recv.at[step], sibling)

    def route(step):
        peer = lax.rem(expert + step, experts)
        return remote(send_ref.at[peer], landed.at[expert], tok_send.at[peer], tok_recv.at[expert], {"expert": peer})

    def landing(source):
        return remote(send_ref.at[source], landed.at[source], tok_send.at[source], tok_recv.at[source], {"expert": source})

    def upward(kind, side):
        return kind == side

    def chunk(kind, side, distance):
        return lax.rem(me + (distance if upward(kind, side) else count - distance), count)

    def place(kind, index):
        return coeff_all.at[0, index] if kind == 0 else raw_all.at[index]

    def ring(src, dst, kind, side, turn):
        return remote(src, dst, ring_send.at[kind, side, turn], ring_recv.at[kind, side, turn],
                      after if upward(kind, side) else before)

    def first(kind, side):
        return ring(parts[kind].at[chunk(kind, side, reach[side])], slots[kind].at[side, 0], kind, side, 0)

    def add_on(kind, side, turn):
        return ring(slots[kind].at[side, turn - 1], slots[kind].at[side, turn], kind, side, turn)

    def pass_on(kind, side, hop):
        here = place(kind, lax.rem(me + (count - hop if upward(kind, side) else hop), count))
        return ring(here, here, kind, side, longer + hop)

    def share(index):
        return remote(coeff_all.at[0, index], coeff_all.at[1, index], share_send.at[index], share_recv.at[index], sibling)

    def serve(kind, turn):
        for side in range(2):
            @pl.when(turn < reach[side])
            def _():
                slot = slots[kind].at[side, turn]
                ring(slot, slot, kind, side, turn).wait_recv()

            @pl.when(turn < reach[side] - 1)
            def _():
                value = parts[kind][chunk(kind, side, reach[side] - 1 - turn)].astype(jnp.float32)
                slots[kind][side, turn] = (slots[kind][side, turn].astype(jnp.float32) + value).astype(jnp.bfloat16)
                add_on(kind, side, turn + 1).start()

        @pl.when(turn == longer - 1)
        def _():
            value = parts[kind][me].astype(jnp.float32) + slots[kind][0, longer - 1].astype(jnp.float32)
            value = value + slots[kind][1, longer - 2].astype(jnp.float32)
            place(kind, me)[...] = value.astype(jnp.bfloat16)
            for side in range(2):
                pass_on(kind, side, 0).start()
            if kind == 0:
                share(me).start()

        hop = turn - longer
        for side in range(2):
            index = lax.rem(me + (2 * count - 1 - hop if upward(kind, side) else hop + 1), count)

            @pl.when((hop >= 0) & (hop < reach[side]))
            def _():
                ring(place(kind, index), place(kind, index), kind, side, turn).wait_recv()
                if kind == 0:
                    share(index).start()

            @pl.when((hop >= 0) & (hop < reach[side] - 1))
            def _():
                pass_on(kind, side, hop + 1).start()

    down = remote(down_ref, other, down_send, down_recv, sibling)
    order = [4, 3, 5, 2, 6, 1, 7]
    for step in order:
        scatter(step).start()

    def route_all(step, carry):
        route(step).start()
        return carry

    lax.fori_loop(1, experts, route_all, 0)
    down.start()
    landed[expert] = send_ref[expert]
    turned = (((0,), (0,)), ((), ()))
    for pick, rows_ref in enumerate((gate_ref, up_ref)):
        block = lax.dot_general(sum_ref[...], rows_ref[...], turned, preferred_element_type=jnp.float32)
        for piece in range(count):
            coeff_part[piece, pick] = block[piece * height:(piece + 1) * height].astype(jnp.bfloat16)
    total = part_ref[me]
    for step in reversed(order):
        scatter(step).wait_recv()
        total = total + arrive[step]
    pieces[half * count + me] = total
    for step in order:
        spread(step).start()
    hand(0).start()
    for side in range(2):
        first(0, side).start()
    for step in reversed(order):
        spread(step).wait_recv()
        hand(step).start()
    for step in range(count):
        hand(step).wait_recv()
    for side in range(2):
        for piece in range(count):
            work[piece * height:(piece + 1) * height, side * width:(side + 1) * width] = pieces[side * count + piece]

    def settle(step, carry):
        landing(lax.rem(expert + step, experts)).wait_recv()
        return carry

    group = raw_part.shape[1] // capacity

    def project(index, carry):
        rows = jnp.concatenate([landed[index * group + item].astype(jnp.float32) for item in range(group)], axis=0)
        raw_part[index] = jnp.dot(
            rows.astype(jnp.bfloat16), sum_ref[...], preferred_element_type=jnp.float32).astype(jnp.bfloat16)
        return carry

    def service(kind, turn):
        if kind == 0:
            serve(0, turn)
        else:
            @pl.when(turn == 1)
            def _():
                lax.fori_loop(1, experts, settle, 0)
                lax.fori_loop(0, experts // group, project, 0)
                for side in range(2):
                    first(1, side).start()

            @pl.when(turn >= 2)
            def _():
                serve(1, turn - 2)

    eliminate(work, inv_ref, service)
    serve(1, count - 2)
    high = work[...].astype(jnp.bfloat16)
    high_ref[...] = high
    low_ref[...] = (work[...] - high.astype(jnp.float32)).astype(jnp.bfloat16)

    def gathered(index, carry):
        share(index).wait_recv()
        return carry

    lax.fori_loop(0, count, gathered, 0)
    down.wait_recv()
    low = low_ref[...]
    for index in range(4):
        side, pick = divmod(index, 2)
        block = jnp.concatenate([coeff_all[side, piece, pick] for piece in range(count)], axis=0)
        final[index] = (jnp.dot(high, block, preferred_element_type=jnp.float32)
                        + jnp.dot(low, block, preferred_element_type=jnp.float32)).astype(jnp.bfloat16)

    serve(1, count - 1)

    def give(target):
        return remote(answers.at[target], back_ref.at[expert], ans_send.at[target], ans_recv.at[expert], {"expert": target})

    def take(source):
        return remote(back_ref.at[source], back_ref.at[source], ans_send.at[source], ans_recv.at[source], {"expert": source})

    dims = (((1,), (1,)), ((), ()))
    groups = experts // GROUP
    span = GROUP * capacity
    each = span // raw_all.shape[1]

    def compute(turn, carry):
        block = lax.rem(expert // GROUP + turn, groups)
        rows = jnp.concatenate([raw_all[block * each + item] for item in range(each)], axis=0)
        projected = (lax.dot_general(rows, high_ref[...], dims, preferred_element_type=jnp.float32)
                     + lax.dot_general(rows, low_ref[...], dims, preferred_element_type=jnp.float32)).astype(jnp.bfloat16)
        result = jnp.zeros((span, depth), jnp.float32)
        for side, rows_ref in enumerate((down_ref, other)):
            gate = jnp.dot(projected, final[2 * side], preferred_element_type=jnp.float32)
            up = jnp.dot(projected, final[2 * side + 1], preferred_element_type=jnp.float32)
            hidden = (gate / (1.0 + jnp.exp(-gate)) * up).astype(jnp.bfloat16)
            result = result + jnp.dot(hidden, rows_ref[...], preferred_element_type=jnp.float32)
        for index in range(GROUP):
            target = block * GROUP + index
            value = result[index * capacity:(index + 1) * capacity].astype(jnp.bfloat16)

            @pl.when(target == expert)
            def _():
                back_ref[expert] = value

            @pl.when(target != expert)
            def _():
                answers[target] = value
                give(target).start()
        return carry

    lax.fori_loop(0, groups, compute, 0)
    for step in order:
        scatter(step).wait_send()
        spread(step).wait_send()
    for step in range(count):
        hand(step).wait_send()
        share(step).wait_send()
    down.wait_send()
    for kind in range(2):
        for side in range(2):
            first(kind, side).wait_send()
            for turn in range(1, reach[side]):
                add_on(kind, side, turn).wait_send()
            for hop in range(reach[side]):
                pass_on(kind, side, hop).wait_send()

    def drain(step, carry):
        route(step).wait_send()
        take(lax.rem(expert + step, experts)).wait_recv()
        give(lax.rem(expert + step, experts)).wait_send()
        return carry

    lax.fori_loop(1, experts, drain, 0)


def expert_answers(part, down, outgoing, summed, gate, up):
    count, height, width = part.shape
    size = count * height
    experts, capacity, depth = outgoing.shape
    hidden = gate.shape[1]
    rows = experts * capacity // count
    low, full = jnp.bfloat16, jnp.float32
    dma = pltpu.SemaphoreType.DMA
    return pl.pallas_call(
        whole_kernel,
        out_shape=jax.ShapeDtypeStruct(outgoing.shape, low),
        in_specs=[pl.BlockSpec(memory_space=pltpu.VMEM)] * 6,
        out_specs=pl.BlockSpec(memory_space=pltpu.VMEM),
        scratch_shapes=[
            pltpu.VMEM((count, height, width), full),
            pltpu.VMEM((2 * count, height, width), full),
            pltpu.VMEM((experts, capacity, depth), low),
            pltpu.VMEM(down.shape, low),
            pltpu.VMEM((count, 2, height, hidden), low),
            pltpu.VMEM((count, rows, size), low),
            pltpu.VMEM((size, size), full),
            pltpu.VMEM((BLK, BLK), full),
            pltpu.VMEM((2, count // 2, 2, height, hidden), low),
            pltpu.VMEM((2, count // 2, rows, size), low),
            pltpu.VMEM((size, size), low),
            pltpu.VMEM((size, size), low),
            pltpu.VMEM((2, count, 2, height, hidden), low),
            pltpu.VMEM((count, rows, size), low),
            pltpu.VMEM((4, size, hidden), low),
            pltpu.VMEM((experts, capacity, depth), low),
        ] + [dma((count,))] * 6 + [dma] * 2 + [dma((experts,))] * 2 + [dma((2, 2, count))] * 2 + [dma((count,))] * 2
        + [dma((experts,))] * 2,
        compiler_params=pltpu.CompilerParams(collective_id=1, has_side_effects=True),
        cost_estimate=pl.CostEstimate(flops=10 ** 11, bytes_accessed=8 * size * size, transcendentals=0),
    )(part, down, outgoing, summed, gate, up)


def transposed_dot(left, right):
    return lax.dot_general(left, right, (((0,), (0,)), ((), ())), preferred_element_type=jnp.float32)


def on_device(tokens, gate_weight, up_weight, down_weight, sketch, clusters, routes, route_weights):
    gate_rows = gate_weight[0]
    up_rows = up_weight[0]
    experts = lax.axis_size("expert")
    tensors = lax.axis_size("tensor")
    half = lax.axis_index("dp")
    sketched = jnp.dot(gate_rows, sketch[0, 0], preferred_element_type=jnp.float32) + jnp.dot(
        up_rows, sketch[0, 1], preferred_element_type=jnp.float32
    )
    rank = sketched.shape[1]

    summed = cluster_sum(sketched, clusters)

    tok_rows, width = tokens.shape
    top_count = routes.shape[1]
    capacity = tok_rows * top_count * 3 // (2 * experts)
    named = routes.T[None] == jnp.arange(experts, dtype=jnp.int32)[:, None, None]
    chosen = jnp.any(named, axis=1)
    shares = jnp.sum(jnp.where(named, route_weights.T[None], 0.0), axis=1)
    token_index = jnp.arange(tok_rows)
    earlier = (token_index[:, None] < token_index[None, :]).astype(jnp.bfloat16)
    place = jnp.dot(chosen.astype(jnp.bfloat16), earlier, preferred_element_type=jnp.float32).astype(jnp.int32)
    holds = chosen[:, None, :] & (place[:, None, :] == jnp.arange(capacity, dtype=jnp.int32)[None, :, None])
    select = holds.astype(jnp.bfloat16).reshape(experts * capacity, tok_rows)
    outgoing = jnp.dot(select, tokens, preferred_element_type=jnp.float32).astype(jnp.bfloat16)
    outgoing = outgoing.reshape(experts, capacity, width)

    columns = lax.dynamic_slice_in_dim(summed, half * (rank // 2), rank // 2, 1)
    gram = transposed_dot(summed, columns).reshape(tensors, rank // tensors, rank // 2)
    returned = expert_answers(gram, down_weight[0], outgoing, summed, gate_rows, up_rows)
    returned = returned.reshape(experts * capacity, width)
    mixing = jnp.where(holds, shares[:, None, :], 0.0).reshape(experts * capacity, tok_rows)
    high = mixing.astype(jnp.bfloat16)
    low = (mixing - high.astype(jnp.float32)).astype(jnp.bfloat16)
    return (transposed_dot(high, returned) + transposed_dot(low, returned)).astype(jnp.bfloat16)


def solution(mesh):
    return jax.shard_map(
        on_device,
        mesh=mesh,
        in_specs=(
            P(("expert", "dp"), "tensor"),
            P("expert", "tensor", "dp"),
            P("expert", "tensor", "dp"),
            P("expert", "dp", "tensor"),
            P("expert", None, "dp", None),
            P(),
            P(("expert", "dp"), None),
            P(("expert", "dp"), None),
        ),
        out_specs=P(("expert", "dp"), "tensor"),
        check_vma=False,
    )
```
